32 devices in a mesh: scen: 4 (over x, core), wide: 8 (over z, y).
Axes of the slice: x: 2, y: 2, z: 4, core: 2. Of those that a mesh axis runs over, the one named last changes fastest.
Arguments:
- hess_scen: float32 [32, 512, 512], P(('scen', 'wide')), may hold values from -1.5 to 5.5, as said below
- upper_flags: int32 [32, 512], P(('scen', 'wide')), may hold values 0 or 1
- lower_dual: float32 [32, 512], P(('scen', 'wide')), may hold values from 0.1 to 10
- lower_slack: float32 [32, 512], P(('scen', 'wide')), may hold values from 0.1 to 10
- upper_dual: float32 [32, 512], P(('scen', 'wide')), may hold values from 0.1 to 10
- upper_slack: float32 [32, 512], P(('scen', 'wide')), may hold values from 0.1 to 10
- coupling: float32 [32, 512, 768], P(('scen', 'wide')), may hold values from -0.25 to 0.25
- pattern: int32 [32, 32], P(('scen', 'wide')), may hold values 0 or 1
- region: int32 [32], P(('scen', 'wide')), may hold values from 0 to 31
- hess_first: float32 [768, 768], P('wide'), may hold values from -1.5 to 5.5, as said below
Outputs:
- scen_factor: float32 [32, 512, 512], P(('scen', 'wide'))
- first_factor: float32 [768, 768], P('wide')
The draws below stay inside these ranges and needn't reach their ends.
Inputs may be any that keep to these rules, and one draw needn't show every extreme that they name: `hess_scen`: each scenario's block is symmetric positive definite. `hess_first`: symmetric positive definite.
All inputs are finite; a program needn't handle non-finite values. No bound on the sum of `upper_flags` or of `pattern` on one device may be relied on, other than what follows from the above.
Results may differ from the reference program's by a relative error of at most 0.0003.
Values sent between devices are 32-bit elements; how exact they have to be, the bound alone decides.
No kernel may reach another device: no remote copies, remote signals or barrier semaphores. Data moves between devices by JAX's collectives and lax.ppermute only.
A program may use at most 64 MiB of HBM per device.

```python
import math
import jax
import jax.numpy as jnp
from jax import lax

NS = 512
N0 = 768
NB = 32
SCEN = 32


def symmetric_blocks(raw, order):
    sym = (raw + jnp.swapaxes(raw, -1, -2)) / math.sqrt(2.0 * order)
    return sym + 4.0 * jnp.eye(order, dtype=jnp.float32)


def draw_hess_scen(key, part):
    key = jax.random.fold_in(key, 11)
    raw = jnp.clip(jax.random.normal(key, (SCEN, NS, NS), jnp.float32), -4.0, 4.0)
    return symmetric_blocks(raw, NS)


def draw_hess_first(key, part):
    key = jax.random.fold_in(key, 23)
    raw = jnp.clip(jax.random.normal(key, (N0, N0), jnp.float32), -4.0, 4.0)
    return symmetric_blocks(raw, N0)


def plant(drawn, rng, smallest, largest):
    longest = drawn.shape.index(max(drawn.shape))
    spots = []
    for shift in (0, 1):
        where = [jax.random.randint(jax.random.fold_in(rng, axis), (), 0, length) for axis, length in enumerate(drawn.shape)]
        where[longest] = (where[longest] + shift) % drawn.shape[longest]
        spots.append(tuple(where))
    return drawn.at[spots[0]].set(smallest).at[spots[1]].set(largest)


def shard_levels(own_key, shape, cuts, least, top_value):
    loudness = 1.0
    for position, blocks in cuts:
        heights = jax.random.uniform(jax.random.fold_in(jax.random.fold_in(own_key, 6), position), (blocks,), jnp.float32, least / len(cuts), top_value / len(cuts))
        loudness = loudness * jnp.repeat(jnp.exp(heights), shape[position] // blocks).reshape((-1,) + (1,) * (len(shape) - 1 - position))
    return loudness


def bell_draw(rng, shape, deviation, bound, split=(), kind=jnp.bfloat16):
    result = deviation * jax.random.normal(rng, shape, jnp.float32)
    if split:
        result = result * shard_levels(rng, shape, split, -0.22, 0.18)
    return jnp.clip(result, -bound, bound).astype(kind)


def setup_inputs(seed: int = 0) -> dict:
    key_list = jax.random.split(jax.random.key(seed), 11)
    return {
        "hess_scen": draw_hess_scen(jax.random.fold_in(key_list[10], 71), 0),
        "upper_flags": plant((jax.random.randint(key_list[1], (SCEN, NS), 0, 2) < 1).astype(jnp.int32), jax.random.fold_in(key_list[1], 1), 0, 1),
        "lower_dual": jnp.clip(jnp.exp(math.log(10.0) - 4.6051702 * jax.random.uniform(key_list[2], (SCEN, NS), jnp.float32) ** shard_levels(key_list[2], (SCEN, NS), ((0, 32),), -0.2, 0.2)), 0.1, 10.0),
        "lower_slack": jnp.clip(jnp.exp(math.log(10.0) - 4.6051702 * jax.random.uniform(key_list[3], (SCEN, NS), jnp.float32) ** shard_levels(key_list[3], (SCEN, NS), ((0, 32),), -0.2, 0.2)), 0.1, 10.0),
        "upper_dual": jnp.clip(jnp.exp(math.log(10.0) - 4.6051702 * jax.random.uniform(key_list[4], (SCEN, NS), jnp.float32) ** shard_levels(key_list[4], (SCEN, NS), ((0, 32),), -0.2, 0.2)), 0.1, 10.0),
        "upper_slack": jnp.clip(jnp.exp(math.log(10.0) - 4.6051702 * jax.random.uniform(key_list[5], (SCEN, NS), jnp.float32) ** shard_levels(key_list[5], (SCEN, NS), ((0, 32),), -0.2, 0.2)), 0.1, 10.0),
        "coupling": bell_draw(key_list[6], (SCEN, NS, N0), NS ** -0.5, 0.25, ((0, 32),), jnp.float32),
        "pattern": plant((jax.random.randint(key_list[7], (SCEN, NB), 0, 16) < 1).astype(jnp.int32), jax.random.fold_in(key_list[7], 1), 0, 1),
        "region": plant(jax.random.randint(key_list[8], (SCEN,), 0, NB), jax.random.fold_in(key_list[8], 1), 0, NB - 1).astype(jnp.int32),
        "hess_first": draw_hess_first(jax.random.fold_in(key_list[10], 71), 0),
    }


def reference(hess_scen, upper_flags, lower_dual, lower_slack, upper_dual, upper_slack, coupling, pattern, region, hess_first):
    width = N0 // NB

    def one_scenario(total, pieces):
        hess, flags, low_d, low_s, up_d, up_s, coup, pat, home = pieces
        barrier = low_d / low_s + flags.astype(jnp.float32) * up_d / up_s
        factor = jnp.linalg.cholesky(hess + jnp.diag(barrier))
        coupled = jnp.maximum(pat, (jnp.arange(NB, dtype=jnp.int32) == home).astype(jnp.int32))
        column_mask = jnp.repeat(coupled.astype(jnp.float32), width)
        solved = jax.scipy.linalg.solve_triangular(factor, coup * column_mask[None, :], lower=True)
        total = total + jnp.dot(solved.T.astype(jnp.float32), solved.astype(jnp.float32), precision=lax.Precision.HIGHEST, preferred_element_type=jnp.float32)
        return (total, factor)
    schur, factors = lax.scan(one_scenario, hess_first, (hess_scen, upper_flags, lower_dual, lower_slack, upper_dual, upper_slack, coupling, pattern, region))
    first_factor = jnp.tril(jnp.linalg.cholesky(schur))
    return (factors, first_factor)
```

```python
import functools
import jax
import jax.numpy as jnp
from jax import lax
from jax.experimental import pallas as pl
from jax.experimental.pallas import tpu as pltpu
from jax.sharding import PartitionSpec as P

T = 128
Q = 32
F32 = jnp.float32
BF = jnp.bfloat16


def split(x):
    hi = x.astype(BF)
    return hi, (x - hi.astype(F32)).astype(BF)


def dot3(a, b, dims):
    ah, al = a
    bh, bl = b
    d = functools.partial(lax.dot_general, dimension_numbers=(dims, ((), ())), preferred_element_type=F32)
    return d(ah, bh) + (d(ah, bl) + d(al, bh))


NN = ((1,), (0,))
NT = ((1,), (1,))
TN = ((0,), (0,))


def row_splat(v, j):
    return jnp.broadcast_to(v[j : j + 1, :], v.shape)


def lane_splat(v, c):
    return jnp.broadcast_to(v[:, c : c + 1], (8, T))


def recip(p):
    r = pl.reciprocal(p, approx=True)
    return r * (2.0 - p * r)


def eliminate(rows, lane0):
    sub = lax.broadcasted_iota(jnp.int32, (8, T), 0)
    n = len(rows)
    v = [[r[:, i : i + T] for i in range(0, r.shape[1], T)] for r in rows]
    b = [[lane_splat(v[h][0], lane0 + c) for c in range(8 * (h + 1))] for h in range(n)]
    out = []
    for g in range(n):
        pivots = jnp.zeros((8, T), F32)
        for jj in range(8):
            j = 8 * g + jj
            pivot = row_splat(b[g][j], jj)
            inv = recip(pivot)
            pivots = jnp.where(sub == jj, pivot, pivots)
            top = [row_splat(w, jj) for w in v[g]]
            across = {c: row_splat(b[c // 8][j], c % 8) for c in range(j + 1, 8 * n)}
            for h in range(g, n):
                m = b[h][j] * inv
                if h == g:
                    m = jnp.where(sub > jj, m, 0.0)
                for c in range(j + 1, 8 * (h + 1)):
                    b[h][c] = b[h][c] - m * across[c]
                v[h] = [w - m * t for w, t in zip(v[h], top)]
        scale = lax.rsqrt(pivots)
        out.append(jnp.concatenate([w * scale for w in v[g]], axis=1))
    return out


def factor_block(d_ref):
    for s in range(T // Q):
        rows = [d_ref[pl.ds(Q * s + 8 * h, 8), :] for h in range(Q // 8)]
        done = jnp.concatenate(eliminate(rows, Q * s), axis=0)
        d_ref[pl.ds(Q * s, Q), :] = done
        if s + 1 < T // Q:
            hi, lo = split(done)
            left = jnp.concatenate([hi[:, :T], hi[:, :T], lo[:, :T]], axis=0)
            right = jnp.concatenate([hi, lo, hi], axis=0)
            change = lax.dot_general(left, right, (TN, ((), ())), preferred_element_type=F32)
            below = pl.ds(Q * (s + 1), T - Q * (s + 1))
            d_ref[below, :] = d_ref[below, :] - change[Q * (s + 1) :, :]


def unit_block():
    r = lax.broadcasted_iota(jnp.int32, (T, T), 0)
    c = lax.broadcasted_iota(jnp.int32, (T, T), 1)
    return r, c


def lower_of(d_ref):
    r, c = unit_block()
    return jnp.where(c >= r, d_ref[:, :T], 0.0).T


def scenario_kernel(
    spot, region, hess, flags, low_d, low_s, up_d, up_s, coup, pattern, first,
    factor, gram, d_ref, lh, ll, xh, xl, whole,
):
    n, m = coup.shape
    nt, mt = n // T, m // T
    r, c = unit_block()
    eye = r == c
    barrier = low_d[...] / low_s[...] + flags[...].astype(F32) * up_d[...] / up_s[...]
    nb = pattern.shape[1]
    width = m // nb
    home = (lax.broadcasted_iota(jnp.int32, (1, nb), 1) == region[0]).astype(jnp.int32)
    coupled = jnp.maximum(pattern[...], home).astype(F32)
    block_row = lax.broadcasted_iota(jnp.int32, (nb, m), 0)
    column = lax.broadcasted_iota(jnp.int32, (nb, m), 1)
    spread = jnp.where((column >= block_row * width) & (column < (block_row + 1) * width), 1.0, 0.0)
    mask = jnp.dot(jnp.broadcast_to(coupled, (8, nb)), spread, preferred_element_type=F32)[0:1, :]

    def step(t, _):
        for k in range(nt):

            @pl.when(t == k)
            def _():
                lo, hi = k * T, (k + 1) * T
                panel = hess[lo:, lo:hi]
                if k:
                    panel = panel - dot3((lh[lo:, :lo], ll[lo:, :lo]), (lh[lo:hi, :lo], ll[lo:hi, :lo]), NT)
                d_ref[:, :T] = panel[:T] + jnp.where(eye, barrier[:, lo:hi], 0.0)
                d_ref[:, T:] = jnp.where(eye, 1.0, 0.0)
                if k + 1 < nt:
                    factor[hi:, lo:hi] = panel[T:]
                    factor[lo:hi, hi:] = jnp.zeros((T, n - hi), F32)

        factor_block(d_ref)
        for k in range(nt):

            @pl.when(t == k)
            def _():
                lo, hi = k * T, (k + 1) * T
                factor[lo:hi, lo:hi] = lower_of(d_ref)
                inv = split(d_ref[:, T:])
                if k + 1 < nt:
                    below = dot3(split(factor[hi:, lo:hi]), inv, NT)
                    factor[hi:, lo:hi] = below
                    lh[hi:, lo:hi], ll[hi:, lo:hi] = split(below)
                rhs = coup[lo:hi, :] * mask
                if k:
                    rhs = rhs - dot3((lh[lo:hi, :lo], ll[lo:hi, :lo]), (xh[:lo], xl[:lo]), NN)
                xh[lo:hi], xl[lo:hi] = split(dot3(inv, split(rhs), NN))

        return 0

    lax.fori_loop(0, nt, step, 0)
    for j in range(0, m, 2 * T):
        a = (xh[:, j:], xl[:, j:])
        b = (xh[:, j : j + 2 * T], xl[:, j : j + 2 * T])
        whole[j:, j : j + 2 * T] = dot3(a, b, TN)

    @pl.when(spot[0] == 0)
    def _():
        own = first.shape[0]
        at = pl.ds(pl.multiple_of(spot[1] * own, 8), own)
        whole[at, :] = whole[at, :] + first[...]

    row = 0
    for j in range(mt):
        count = m - j * T
        gram[row : row + count, :] = whole[j * T :, j * T : (j + 1) * T]
        row += count
    if row < gram.shape[0]:
        gram[row:, :] = jnp.zeros((gram.shape[0] - row, T), F32)


def first_kernel(spot, packed, out, d_ref, panel_ref, lh, ll, full):
    m = full.shape[0]
    mt = m // T
    r, c = unit_block()
    eye = r == c
    start = [sum(m - i * T for i in range(j)) for j in range(mt)]

    def step(t, _):
        for k in range(mt):

            @pl.when(t == k)
            def _():
                lo, hi = k * T, (k + 1) * T
                panel = packed[start[k] : start[k] + m - lo, :]
                if k:
                    panel = panel - dot3((lh[lo:, :lo], ll[lo:, :lo]), (lh[lo:hi, :lo], ll[lo:hi, :lo]), NT)
                d_ref[:, :T] = panel[:T]
                d_ref[:, T:] = jnp.where(eye, 1.0, 0.0)
                if k + 1 < mt:
                    panel_ref[hi:, :] = panel[T:]
                    full[lo:hi, hi:] = jnp.zeros((T, m - hi), F32)

        factor_block(d_ref)
        for k in range(mt):

            @pl.when(t == k)
            def _():
                lo, hi = k * T, (k + 1) * T
                full[lo:hi, lo:hi] = lower_of(d_ref)
                if k + 1 < mt:
                    below = dot3(split(panel_ref[hi:, :]), split(d_ref[:, T:]), NT)
                    full[hi:, lo:hi] = below
                    lh[hi:, lo:hi], ll[hi:, lo:hi] = split(below)

        return 0

    lax.fori_loop(0, mt, step, 0)
    own = out.shape[0]
    out[...] = full[pl.ds(pl.multiple_of(spot[1] * own, 8), own), :]


VMEM = pl.BlockSpec(memory_space=pltpu.VMEM)
SMEM = pl.BlockSpec(memory_space=pltpu.SMEM)


def packed_rows(m, devices):
    rows = sum(m - j * T for j in range(m // T))
    unit = 8 * devices
    return -(-rows // unit) * unit


def scenario(spot, region, hess, flags, low_d, low_s, up_d, up_s, coup, pattern, first, rows):
    n, m = coup.shape
    return pl.pallas_call(
        scenario_kernel,
        out_shape=(jax.ShapeDtypeStruct((n, n), F32), jax.ShapeDtypeStruct((rows, T), F32)),
        in_specs=[SMEM, SMEM] + [VMEM] * 9,
        out_specs=(VMEM, VMEM),
        scratch_shapes=[
            pltpu.VMEM((T, 2 * T), F32),
            pltpu.VMEM((n, n), BF),
            pltpu.VMEM((n, n), BF),
            pltpu.VMEM((n, m), BF),
            pltpu.VMEM((n, m), BF),
            pltpu.VMEM((m, m), F32),
        ],
        name="scenario",
    )(spot, region, hess, flags, low_d, low_s, up_d, up_s, coup, pattern, first)


def first_section(spot, packed, own, m):
    return pl.pallas_call(
        first_kernel,
        out_shape=jax.ShapeDtypeStruct((own, m), F32),
        in_specs=[SMEM, VMEM],
        out_specs=VMEM,
        scratch_shapes=[
            pltpu.VMEM((T, 2 * T), F32),
            pltpu.VMEM((m, T), F32),
            pltpu.VMEM((m, m), BF),
            pltpu.VMEM((m, m), BF),
            pltpu.VMEM((m, m), F32),
        ],
        name="first_section",
    )(spot, packed)


def partner(x, axis, size, bit):
    return lax.ppermute(x, axis, [(i, i ^ bit) for i in range(size)])


def sum_everywhere(x, sizes):
    rounds = [(axis, size, bit) for axis, size in sizes for bit in (1 << k for k in range(size.bit_length() - 1))]
    for axis, size, bit in rounds:
        upper = (lax.axis_index(axis) & bit) != 0
        half = x.shape[0] // 2
        low, high = x[:half], x[half:]
        x = jnp.where(upper, high, low) + partner(jnp.where(upper, low, high), axis, size, bit)
    for axis, size, bit in reversed(rounds):
        upper = (lax.axis_index(axis) & bit) != 0
        other = partner(x, axis, size, bit)
        x = jnp.where(upper, jnp.concatenate([other, x]), jnp.concatenate([x, other]))
    return x


def solution(mesh):
    sizes = [(axis, mesh.shape[axis]) for axis in ("scen", "wide")]
    devices = sizes[0][1] * sizes[1][1]

    def per_device(hess_scen, flags, low_d, low_s, up_d, up_s, coupling, pattern, region, hess_first):
        own, m = hess_first.shape
        rows = packed_rows(m, devices)
        place = [lax.axis_index(axis).astype(jnp.int32) for axis in ("scen", "wide")]
        factors, total = [], None
        for i in range(hess_scen.shape[0]):
            lead = place[0] if i == 0 else jnp.int32(1)
            factor, gram = scenario(
                jnp.stack([lead, place[1]]), region[i : i + 1], hess_scen[i],
                flags[i : i + 1], low_d[i : i + 1], low_s[i : i + 1], up_d[i : i + 1], up_s[i : i + 1],
                coupling[i], pattern[i : i + 1], hess_first, rows,
            )
            factors.append(factor)
            total = gram if total is None else total + gram
        summed = sum_everywhere(total, sizes)
        mine = first_section(jnp.stack(place), summed, own, m)
        return (jnp.stack(factors), mine)

    each = P(("scen", "wide"))
    return jax.shard_map(
        per_device,
        mesh=mesh,
        in_specs=(each,) * 9 + (P("wide", None),),
        out_specs=(each, P("wide", None)),
        check_vma=False,
    )
```

```python
import functools
import jax
import jax.numpy as jnp
from jax import lax
from jax.experimental import pallas as pl
from jax.experimental.pallas import tpu as pltpu
from jax.sharding import PartitionSpec as P

T = 128
Q = 32
F32 = jnp.float32
BF = jnp.bfloat16


def split(x):
    hi = x.astype(BF)
    return hi, (x - hi.astype(F32)).astype(BF)


def dot3(a, b, dims):
    ah, al = a
    bh, bl = b
    d = functools.partial(lax.dot_general, dimension_numbers=(dims, ((), ())), preferred_element_type=F32)
    return d(ah, bh) + (d(ah, bl) + d(al, bh))


NN = ((1,), (0,))
NT = ((1,), (1,))
TN = ((0,), (0,))


def row_splat(v, j):
    return jnp.broadcast_to(v[j : j + 1, :], v.shape)


def lane_splat(v, c):
    return jnp.take_along_axis(v, jnp.full((8, T), c, jnp.int32), axis=1, mode="promise_in_bounds")


def eliminate(rows, lane0):
    sub = lax.broadcasted_iota(jnp.int32, (8, T), 0)
    n = len(rows)
    v = [[r[:, i : i + T] for i in range(0, r.shape[1], T)] for r in rows]
    block = {}

    def fetch(h, k):
        block[h, k] = [lane_splat(v[h][0], lane0 + 8 * k + c) for c in range(8)]

    for h in range(n):
        fetch(h, 0)
    fetch(1, 1)
    out = []
    for g in range(n):
        for h in range(g + 1, n):
            if (h, g) not in block:
                fetch(h, g)
        later = [key for key in block if key[1] > g]
        own = block[g, g]
        pivots = jnp.zeros((8, T), F32)
        pivot = row_splat(own[0], 0)
        for j in range(8):
            pivots = jnp.where(sub == j, pivot, pivots)
            inv = 1.0 / pivot
            if j < 7:
                side = row_splat(own[j], j + 1)
                pivot = row_splat(own[j + 1], j + 1) - (side * side) * inv
            top = [row_splat(w, j) for w in v[g]]
            across = {c: row_splat(own[j], c) for c in range(j + 1, 8)}
            far = {k: [row_splat(block[k, g][j], c) for c in range(8)] for k in sorted({key[1] for key in later})}
            m = {}
            for h in range(g, n):
                here = block[h, g]
                m[h] = here[j] * inv
                for c in range(j + 1, 8):
                    here[c] = here[c] - m[h] * across[c]
            for h, k in later:
                there = block[h, k]
                for c in range(8):
                    there[c] = there[c] - m[h] * far[k][c]
            for h in range(g, n):
                part = jnp.where(sub > j, m[h], 0.0) if h == g else m[h]
                v[h] = [w - part * t for w, t in zip(v[h], top)]
        scale = lax.rsqrt(pivots)
        out.append(jnp.concatenate([w * scale for w in v[g]], axis=1))
        for h in range(g + 2, n):
            for k in (g + 1, g + 2):
                if k <= h and (h, k) not in block:
                    fetch(h, k)
    return out


def factor_block(d_ref):
    for s in range(T // Q):
        rows = [d_ref[pl.ds(Q * s + 8 * h, 8), :] for h in range(Q // 8)]
        done = jnp.concatenate(eliminate(rows, Q * s), axis=0)
        d_ref[pl.ds(Q * s, Q), :] = done
        if s + 1 < T // Q:
            hi, lo = split(done)
            left = jnp.concatenate([hi[:, :T], hi[:, :T], lo[:, :T]], axis=0)
            right = jnp.concatenate([hi, lo, hi], axis=0)
            change = lax.dot_general(left, right, (TN, ((), ())), preferred_element_type=F32)
            below = pl.ds(Q * (s + 1), T - Q * (s + 1))
            d_ref[below, :] = d_ref[below, :] - change[Q * (s + 1) :, :]


def unit_block():
    r = lax.broadcasted_iota(jnp.int32, (T, T), 0)
    c = lax.broadcasted_iota(jnp.int32, (T, T), 1)
    return r, c


def lower_of(d_ref):
    r, c = unit_block()
    return jnp.where(c >= r, d_ref[:, :T], 0.0).T


def scenario_kernel(
    count, spot, region, hess, flags, low_d, low_s, up_d, up_s, coup, pattern, first,
    factor, gram, d_ref, lh, ll, xh, xl, whole,
):
    n, m = coup.shape
    nt, mt = n // T, m // T
    r, c = unit_block()
    eye = r == c
    barrier = low_d[...] / low_s[...] + flags[...].astype(F32) * up_d[...] / up_s[...]
    nb = pattern.shape[1]
    width = m // nb
    home = (lax.broadcasted_iota(jnp.int32, (1, nb), 1) == region[0]).astype(jnp.int32)
    coupled = jnp.maximum(pattern[...], home).astype(F32)
    block_row = lax.broadcasted_iota(jnp.int32, (nb, m), 0)
    column = lax.broadcasted_iota(jnp.int32, (nb, m), 1)
    spread = jnp.where((column >= block_row * width) & (column < (block_row + 1) * width), 1.0, 0.0)
    mask = jnp.dot(jnp.broadcast_to(coupled, (8, nb)), spread, preferred_element_type=F32)[0:1, :]

    def step(t, _):
        for k in range(nt):

            @pl.when(t == k)
            def _():
                lo, hi = k * T, (k + 1) * T
                panel = hess[lo:, lo:hi]
                if k:
                    panel = panel - dot3((lh[lo:, :lo], ll[lo:, :lo]), (lh[lo:hi, :lo], ll[lo:hi, :lo]), NT)
                d_ref[:, :T] = panel[:T] + jnp.where(eye, barrier[:, lo:hi], 0.0)
                d_ref[:, T:] = jnp.where(eye, 1.0, 0.0)
                if k + 1 < nt:
                    factor[hi:, lo:hi] = panel[T:]
                    factor[lo:hi, hi:] = jnp.zeros((T, n - hi), F32)

        factor_block(d_ref)
        for k in range(nt):

            @pl.when(t == k)
            def _():
                lo, hi = k * T, (k + 1) * T
                factor[lo:hi, lo:hi] = lower_of(d_ref)
                inv = split(d_ref[:, T:])
                if k + 1 < nt:
                    below = dot3(split(factor[hi:, lo:hi]), inv, NT)
                    factor[hi:, lo:hi] = below
                    lh[hi:, lo:hi], ll[hi:, lo:hi] = split(below)
                rhs = coup[lo:hi, :] * mask
                if k:
                    rhs = rhs - dot3((lh[lo:hi, :lo], ll[lo:hi, :lo]), (xh[:lo], xl[:lo]), NN)
                xh[lo:hi], xl[lo:hi] = split(dot3(inv, split(rhs), NN))

        return 0

    lax.fori_loop(0, nt, step, 0)
    for j in range(0, m, 2 * T):
        a = (xh[:, j:], xl[:, j:])
        b = (xh[:, j : j + 2 * T], xl[:, j : j + 2 * T])
        whole[j:, j : j + 2 * T] = dot3(a, b, TN)

    @pl.when(spot[0] == 0)
    def _():
        own = first.shape[0]
        at = pl.ds(pl.multiple_of(spot[1] * own, 8), own)
        whole[at, :] = whole[at, :] + first[...]

    chunk = gram.shape[0] // count
    for l, at, rows, i, j in pieces(m, gram.shape[0], count):
        to = pl.multiple_of((spot[2] ^ l) * chunk, 8) + at
        if i is None:
            gram[pl.ds(to, rows), :] = jnp.zeros((rows, T), F32)
        else:
            gram[pl.ds(to, rows), :] = whole[i : i + rows, j : j + T]


def first_kernel(count, spot, *refs):
    parts, (out, d_ref, panel_ref, lh, ll, full, packed) = refs[:-7], refs[-7:]
    m = full.shape[0]
    mt = m // T
    r, c = unit_block()
    eye = r == c
    start = [sum(m - i * T for i in range(j)) for j in range(mt)]
    chunk = packed.shape[0] // count
    each = count // len(parts)
    for p in range(count):
        to = pl.multiple_of((spot[2] ^ p) * chunk, 8)
        at = (p % each) * chunk
        packed[pl.ds(to, chunk), :] = parts[p // each][at : at + chunk, :]

    def step(t, _):
        for k in range(mt):

            @pl.when(t == k)
            def _():
                lo, hi = k * T, (k + 1) * T
                panel = packed[start[k] : start[k] + m - lo, :]
                if k:
                    panel = panel - dot3((lh[lo:, :lo], ll[lo:, :lo]), (lh[lo:hi, :lo], ll[lo:hi, :lo]), NT)
                d_ref[:, :T] = panel[:T]
                d_ref[:, T:] = jnp.where(eye, 1.0, 0.0)
                if k + 1 < mt:
                    panel_ref[hi:, :] = panel[T:]
                    full[lo:hi, hi:] = jnp.zeros((T, m - hi), F32)

        factor_block(d_ref)
        for k in range(mt):

            @pl.when(t == k)
            def _():
                lo, hi = k * T, (k + 1) * T
                full[lo:hi, lo:hi] = lower_of(d_ref)
                if k + 1 < mt:
                    below = dot3(split(panel_ref[hi:, :]), split(d_ref[:, T:]), NT)
                    full[hi:, lo:hi] = below
                    lh[hi:, lo:hi], ll[hi:, lo:hi] = split(below)

        return 0

    lax.fori_loop(0, mt, step, 0)
    own = out.shape[0]
    out[...] = full[pl.ds(pl.multiple_of(spot[1] * own, 8), own), :]


VMEM = pl.BlockSpec(memory_space=pltpu.VMEM)
SMEM = pl.BlockSpec(memory_space=pltpu.SMEM)


def packed_rows(m, devices):
    rows = sum(m - j * T for j in range(m // T))
    unit = 8 * devices
    return -(-rows // unit) * unit


def pieces(m, total, count):
    chunk = total // count
    spans = [(i, j) for j in range(0, m, T) for i in range(j, m, T)]
    cuts = sorted(set(range(0, total, chunk)) | set(range(0, len(spans) * T, T)) | {len(spans) * T, total})
    for lo, hi in zip(cuts, cuts[1:]):
        i, j = spans[lo // T] if lo < len(spans) * T else (None, None)
        yield lo // chunk, lo % chunk, hi - lo, None if i is None else i + lo % T, j


def scenario(spot, region, hess, flags, low_d, low_s, up_d, up_s, coup, pattern, first, rows, count):
    n, m = coup.shape
    return pl.pallas_call(
        functools.partial(scenario_kernel, count),
        out_shape=(jax.ShapeDtypeStruct((n, n), F32), jax.ShapeDtypeStruct((rows, T), F32)),
        in_specs=[SMEM, SMEM] + [VMEM] * 9,
        out_specs=(VMEM, VMEM),
        scratch_shapes=[
            pltpu.VMEM((T, 2 * T), F32),
            pltpu.VMEM((n, n), BF),
            pltpu.VMEM((n, n), BF),
            pltpu.VMEM((n, m), BF),
            pltpu.VMEM((n, m), BF),
            pltpu.VMEM((m, m), F32),
        ],
        name="scenario",
    )(spot, region, hess, flags, low_d, low_s, up_d, up_s, coup, pattern, first)


def first_section(spot, parts, own, m, count):
    rows = sum(part.shape[0] for part in parts)
    return pl.pallas_call(
        functools.partial(first_kernel, count),
        out_shape=jax.ShapeDtypeStruct((own, m), F32),
        in_specs=[SMEM] + [VMEM] * len(parts),
        out_specs=VMEM,
        scratch_shapes=[
            pltpu.VMEM((T, 2 * T), F32),
            pltpu.VMEM((m, T), F32),
            pltpu.VMEM((m, m), BF),
            pltpu.VMEM((m, m), BF),
            pltpu.VMEM((m, m), F32),
            pltpu.VMEM((rows, T), F32),
        ],
        name="first_section",
    )(spot, *parts)


AXES = ("scen", "wide")


def swap(x, mask, count):
    return lax.ppermute(x, AXES, [(i, i ^ mask) for i in range(count)])


def rounds_of(sizes):
    (_, scen), (_, wide) = sizes
    bits = [wide << k for k in range(scen.bit_length() - 1)] + [1 << k for k in range(wide.bit_length() - 1)]
    return [bits[:1]] + [bits[k : k + 2] for k in range(1, len(bits), 2)]


def masks_of(bits):
    return [sum(b for k, b in enumerate(bits) if d >> k & 1) for d in range(1 << len(bits))]


def place_of(flat, rounds):
    bits = [bit for group in reversed(rounds) for bit in group]
    return sum(((flat // bit) % 2) << k for k, bit in enumerate(bits))


def sum_everywhere(x, rounds, count):
    for bits in rounds:
        masks = masks_of(bits)
        part = x.shape[0] // len(masks)
        cut = [x[k * part : (k + 1) * part] for k in range(len(masks))]
        got = [swap(c, mask, count) for c, mask in zip(cut[1:], masks[1:])]
        x = functools.reduce(jnp.add, got, cut[0])
    parts = [x]
    for bits in reversed(rounds):
        x = parts[0] if len(parts) == 1 else jnp.concatenate(parts)
        parts = [x] + [swap(x, mask, count) for mask in masks_of(bits)[1:]]
    return parts


def solution(mesh):
    sizes = [(axis, mesh.shape[axis]) for axis in AXES]
    count = sizes[0][1] * sizes[1][1]
    rounds = rounds_of(sizes)

    def per_device(hess_scen, flags, low_d, low_s, up_d, up_s, coupling, pattern, region, hess_first):
        own, m = hess_first.shape
        rows = packed_rows(m, count)
        scen, wide = [lax.axis_index(axis).astype(jnp.int32) for axis in AXES]
        place = place_of(scen * sizes[1][1] + wide, rounds)
        factors, total = [], None
        for i in range(hess_scen.shape[0]):
            lead = scen if i == 0 else jnp.int32(1)
            factor, gram = scenario(
                jnp.stack([lead, wide, place]), region[i : i + 1], hess_scen[i],
                flags[i : i + 1], low_d[i : i + 1], low_s[i : i + 1], up_d[i : i + 1], up_s[i : i + 1],
                coupling[i], pattern[i : i + 1], hess_first, rows, count,
            )
            factors.append(factor)
            total = gram if total is None else total + gram
        parts = sum_everywhere(total, rounds, count)
        mine = first_section(jnp.stack([scen, wide, place]), parts, own, m, count)
        return (jnp.stack(factors), mine)

    each = P(AXES)
    return jax.shard_map(
        per_device,
        mesh=mesh,
        in_specs=(each,) * 9 + (P("wide", None),),
        out_specs=(each, P("wide", None)),
        check_vma=False,
    )
```

```python
import functools
import jax
import jax.numpy as jnp
from jax import lax
from jax.experimental import pallas as pl
from jax.experimental.pallas import tpu as pltpu
from jax.sharding import PartitionSpec as P

T = 128
Q = 32
F32 = jnp.float32
BF = jnp.bfloat16


def split(x):
    hi = x.astype(BF)
    return hi, (x - hi.astype(F32)).astype(BF)


def dot3(a, b, dims):
    ah, al = a
    bh, bl = b
    d = functools.partial(lax.dot_general, dimension_numbers=(dims, ((), ())), preferred_element_type=F32)
    return d(ah, bh) + (d(ah, bl) + d(al, bh))


NN = ((1,), (0,))
NT = ((1,), (1,))
TN = ((0,), (0,))


def row_splat(v, j):
    return jnp.broadcast_to(v[j : j + 1, :], v.shape)


def lane_splat(v, c):
    return jnp.take_along_axis(v, jnp.full((8, T), c, jnp.int32), axis=1, mode="promise_in_bounds")


def eliminate(rows, lane0):
    sub = lax.broadcasted_iota(jnp.int32, (8, T), 0)
    n = len(rows)
    v = [[r[:, i : i + T] for i in range(0, r.shape[1], T)] for r in rows]
    block = {}

    def fetch(h, k):
        block[h, k] = [lane_splat(v[h][0], lane0 + 8 * k + c) for c in range(8)]

    for h in range(n):
        fetch(h, 0)
    fetch(1, 1)
    out = []
    for g in range(n):
        for h in range(g + 1, n):
            if (h, g) not in block:
                fetch(h, g)
        later = [key for key in block if key[1] > g]
        own = block[g, g]
        pivots = jnp.zeros((8, T), F32)
        pivot = row_splat(own[0], 0)
        for j in range(8):
            pivots = jnp.where(sub == j, pivot, pivots)
            inv = 1.0 / pivot
            if j < 7:
                side = row_splat(own[j], j + 1)
                pivot = row_splat(own[j + 1], j + 1) - (side * side) * inv
            top = [row_splat(w, j) for w in v[g]]
            across = {c: row_splat(own[j], c) for c in range(j + 1, 8)}
            far = {k: [row_splat(block[k, g][j], c) for c in range(8)] for k in sorted({key[1] for key in later})}
            m = {}
            for h in range(g, n):
                here = block[h, g]
                m[h] = here[j] * inv
                for c in range(j + 1, 8):
                    here[c] = here[c] - m[h] * across[c]
            for h, k in later:
                there = block[h, k]
                for c in range(8):
                    there[c] = there[c] - m[h] * far[k][c]
            for h in range(g, n):
                part = jnp.where(sub > j, m[h], 0.0) if h == g else m[h]
                v[h] = [w - part * t for w, t in zip(v[h], top)]
        scale = lax.rsqrt(pivots)
        out.append(jnp.concatenate([w * scale for w in v[g]], axis=1))
        for h in range(g + 2, n):
            for k in (g + 1, g + 2):
                if k <= h and (h, k) not in block:
                    fetch(h, k)
    return out


def factor_block(d_ref):
    for s in range(T // Q):
        rows = [d_ref[pl.ds(Q * s + 8 * h, 8), :] for h in range(Q // 8)]
        done = jnp.concatenate(eliminate(rows, Q * s), axis=0)
        d_ref[pl.ds(Q * s, Q), :] = done
        if s + 1 < T // Q:
            hi, lo = split(done)
            left = jnp.concatenate([hi[:, :T], hi[:, :T], lo[:, :T]], axis=0)
            right = jnp.concatenate([hi, lo, hi], axis=0)
            change = lax.dot_general(left, right, (TN, ((), ())), preferred_element_type=F32)
            below = pl.ds(Q * (s + 1), T - Q * (s + 1))
            d_ref[below, :] = d_ref[below, :] - change[Q * (s + 1) :, :]


def unit_block():
    r = lax.broadcasted_iota(jnp.int32, (T, T), 0)
    c = lax.broadcasted_iota(jnp.int32, (T, T), 1)
    return r, c


def lower_of(d_ref):
    r, c = unit_block()
    return jnp.where(c >= r, d_ref[:, :T], 0.0).T


def scenario_kernel(
    place_fn, count, region, hess_hbm, flags, low_d, low_s, up_d, up_s, coup_hbm, pattern, first,
    factor_hbm, keep, send, hess, coup, factor, d_ref, ih, il, lh, ll, xh, xl, whole, in_sem, out_sem,
):
    n, m = coup.shape
    nt, mt = n // T, m // T
    loads = []
    for k in range(nt):
        cut = (pl.ds(k * T, n - k * T), pl.ds(k * T, T))
        loads.append(pltpu.make_async_copy(hess_hbm.at[cut], hess.at[cut], in_sem.at[k]))
        cut = pl.ds(k * T, T)
        loads.append(pltpu.make_async_copy(coup_hbm.at[cut], coup.at[cut], in_sem.at[nt + k]))
    for load in loads:
        load.start()
    stores = []
    for k in range(nt):
        cut = (slice(None), pl.ds(k * T, T))
        stores.append(pltpu.make_async_copy(factor.at[cut], factor_hbm.at[cut], out_sem.at[k]))
    lead, wide, place = place_fn()
    r, c = unit_block()
    eye = r == c
    barrier = low_d[...] / low_s[...] + flags[...].astype(F32) * up_d[...] / up_s[...]
    nb = pattern.shape[1]
    width = m // nb
    home = (lax.broadcasted_iota(jnp.int32, (1, nb), 1) == region[0]).astype(jnp.int32)
    coupled = jnp.maximum(pattern[...], home).astype(F32)
    block_row = lax.broadcasted_iota(jnp.int32, (nb, m), 0)
    column = lax.broadcasted_iota(jnp.int32, (nb, m), 1)
    spread = jnp.where((column >= block_row * width) & (column < (block_row + 1) * width), 1.0, 0.0)
    mask = jnp.dot(jnp.broadcast_to(coupled, (8, nb)), spread, preferred_element_type=F32)[0:1, :]
    for ref in (lh, ll, xh, xl, ih, il):
        ref[...] = jnp.zeros(ref.shape, BF)

    def solve(t):
        rows = pl.ds(pl.multiple_of(t * T, T), T)
        rhs = coup[rows, :] * mask - dot3((lh[rows, :], ll[rows, :]), (xh[...], xl[...]), NN)
        return rows, dot3((ih[...], il[...]), split(rhs), NN)

    def step(t, _):
        for k in range(nt):

            @pl.when(t == k)
            def _():
                lo, hi = k * T, (k + 1) * T
                loads[2 * k].wait()
                loads[2 * k + 1].wait()
                panel = hess[lo:, lo:hi]
                if k:
                    panel = panel - dot3((lh[lo:, :lo], ll[lo:, :lo]), (lh[lo:hi, :lo], ll[lo:hi, :lo]), NT)
                    factor[:lo, lo:hi] = jnp.zeros((lo, T), F32)
                d_ref[:, :T] = panel[:T] + jnp.where(eye, barrier[:, lo:hi], 0.0)
                d_ref[:, T:] = jnp.where(eye, 1.0, 0.0)
                if k + 1 < nt:
                    factor[hi:, lo:hi] = panel[T:]

        rows, solved = solve(jnp.maximum(t - 1, 0))
        xh[rows, :], xl[rows, :] = split(jnp.where(t > 0, solved, 0.0))
        factor_block(d_ref)
        ih[...], il[...] = split(d_ref[:, T:])
        for k in range(nt):

            @pl.when(t == k)
            def _():
                lo, hi = k * T, (k + 1) * T
                factor[lo:hi, lo:hi] = lower_of(d_ref)
                if k + 1 < nt:
                    below = dot3(split(factor[hi:, lo:hi]), (ih[...], il[...]), NT)
                    factor[hi:, lo:hi] = below
                    lh[hi:, lo:hi], ll[hi:, lo:hi] = split(below)
                stores[k].start()

        return 0

    lax.fori_loop(0, nt, step, 0)
    rows, solved = solve(nt - 1)
    xh[rows, :], xl[rows, :] = split(solved)
    for j in range(0, m, 2 * T):
        a = (xh[:, j:], xl[:, j:])
        b = (xh[:, j : j + 2 * T], xl[:, j : j + 2 * T])
        whole[j:, j : j + 2 * T] = dot3(a, b, TN)

    @pl.when(lead == 0)
    def _():
        own = first.shape[0]
        at = pl.ds(pl.multiple_of(wide * own, 8), own)
        whole[at, :] = whole[at, :] + first[...]

    half = count // 2
    chunk = keep.shape[0] // half
    for side in range(2):

        @pl.when(place // half == side)
        def _():
            for l, at, rows, i, j in pieces(m, count * chunk, count):
                to = pl.multiple_of(((l ^ place) % half) * chunk, 8) + at
                target = (keep, send)[(l // half) ^ side]
                target[pl.ds(to, rows), :] = jnp.zeros((rows, T), F32) if i is None else whole[i : i + rows, j : j + T]

    for store in stores:
        store.wait()


def first_kernel(place_fn, count, *refs):
    _, wide, place = place_fn()
    parts, (out, d_ref, panel_ref, lh, ll, full, packed) = refs[:-7], refs[-7:]
    m = full.shape[0]
    mt = m // T
    r, c = unit_block()
    eye = r == c
    start = [sum(m - i * T for i in range(j)) for j in range(mt)]
    chunk = packed.shape[0] // count
    each = count // len(parts)
    for p in range(count):
        to = pl.multiple_of((place ^ p) * chunk, 8)
        at = (p % each) * chunk
        packed[pl.ds(to, chunk), :] = parts[p // each][at : at + chunk, :]

    def step(t, _):
        for k in range(mt):

            @pl.when(t == k)
            def _():
                lo, hi = k * T, (k + 1) * T
                panel = packed[start[k] : start[k] + m - lo, :]
                if k:
                    panel = panel - dot3((lh[lo:, :lo], ll[lo:, :lo]), (lh[lo:hi, :lo], ll[lo:hi, :lo]), NT)
                d_ref[:, :T] = panel[:T]
                d_ref[:, T:] = jnp.where(eye, 1.0, 0.0)
                if k + 1 < mt:
                    panel_ref[hi:, :] = panel[T:]
                    full[lo:hi, hi:] = jnp.zeros((T, m - hi), F32)

        factor_block(d_ref)
        for k in range(mt):

            @pl.when(t == k)
            def _():
                lo, hi = k * T, (k + 1) * T
                full[lo:hi, lo:hi] = lower_of(d_ref)
                if k + 1 < mt:
                    below = dot3(split(panel_ref[hi:, :]), split(d_ref[:, T:]), NT)
                    full[hi:, lo:hi] = below
                    lh[hi:, lo:hi], ll[hi:, lo:hi] = split(below)

        return 0

    lax.fori_loop(0, mt, step, 0)
    own = out.shape[0]
    out[...] = full[pl.ds(pl.multiple_of(wide * own, 8), own), :]


VMEM = pl.BlockSpec(memory_space=pltpu.VMEM)
SMEM = pl.BlockSpec(memory_space=pltpu.SMEM)
HBM = pl.BlockSpec(memory_space=pltpu.HBM)
GRANT = 24 << 20


def packed_rows(m, devices):
    rows = sum(m - j * T for j in range(m // T))
    unit = 8 * devices
    return -(-rows // unit) * unit


def pieces(m, total, count):
    chunk = total // count
    spans = [(i, j) for j in range(0, m, T) for i in range(j, m, T)]
    cuts = sorted(set(range(0, total, chunk)) | set(range(0, len(spans) * T, T)) | {len(spans) * T, total})
    for lo, hi in zip(cuts, cuts[1:]):
        i, j = spans[lo // T] if lo < len(spans) * T else (None, None)
        yield lo // chunk, lo % chunk, hi - lo, None if i is None else i + lo % T, j


def scenario(place_fn, region, hess, flags, low_d, low_s, up_d, up_s, coup, pattern, first, rows, count):
    n, m = coup.shape
    half = jax.ShapeDtypeStruct((rows // 2, T), F32)
    return pl.pallas_call(
        functools.partial(scenario_kernel, place_fn, count),
        out_shape=(jax.ShapeDtypeStruct((n, n), F32), half, half),
        in_specs=[SMEM, HBM] + [VMEM] * 5 + [HBM, VMEM, VMEM],
        out_specs=(HBM, VMEM, VMEM),
        scratch_shapes=[
            pltpu.VMEM((n, n), F32),
            pltpu.VMEM((n, m), F32),
            pltpu.VMEM((n, n), F32),
            pltpu.VMEM((T, 2 * T), F32),
            pltpu.VMEM((T, T), BF),
            pltpu.VMEM((T, T), BF),
            pltpu.VMEM((n, n), BF),
            pltpu.VMEM((n, n), BF),
            pltpu.VMEM((n, m), BF),
            pltpu.VMEM((n, m), BF),
            pltpu.VMEM((m, m), F32),
            pltpu.SemaphoreType.DMA((2 * n // T,)),
            pltpu.SemaphoreType.DMA((n // T,)),
        ],
        compiler_params=pltpu.CompilerParams(vmem_limit_bytes=GRANT),
        name="scenario",
    )(region, hess, flags, low_d, low_s, up_d, up_s, coup, pattern, first)


def first_section(place_fn, parts, own, m, count):
    rows = sum(part.shape[0] for part in parts)
    return pl.pallas_call(
        functools.partial(first_kernel, place_fn, count),
        out_shape=jax.ShapeDtypeStruct((own, m), F32),
        in_specs=[VMEM] * len(parts),
        out_specs=VMEM,
        scratch_shapes=[
            pltpu.VMEM((T, 2 * T), F32),
            pltpu.VMEM((m, T), F32),
            pltpu.VMEM((m, m), BF),
            pltpu.VMEM((m, m), BF),
            pltpu.VMEM((m, m), F32),
            pltpu.VMEM((rows, T), F32),
        ],
        compiler_params=pltpu.CompilerParams(vmem_limit_bytes=GRANT),
        name="first_section",
    )(*parts)


AXES = ("scen", "wide")


def swap(x, mask, count):
    return lax.ppermute(x, AXES, [(i, i ^ mask) for i in range(count)])


def rounds_of(sizes):
    (_, scen), (_, wide) = sizes
    bits = [wide << k for k in range(scen.bit_length() - 1)] + [1 << k for k in range(wide.bit_length() - 1)]
    return [bits[:1]] + [bits[k : k + 2] for k in range(1, len(bits), 2)]


def masks_of(bits):
    return [sum(b for k, b in enumerate(bits) if d >> k & 1) for d in range(1 << len(bits))]


def place_of(flat, rounds):
    bits = [bit for group in reversed(rounds) for bit in group]
    return sum(((flat // bit) % 2) << k for k, bit in enumerate(bits))


def sum_everywhere(x, sent, rounds, count):
    x = x + swap(sent, masks_of(rounds[0])[1], count)
    for bits in rounds[1:]:
        masks = masks_of(bits)
        part = x.shape[0] // len(masks)
        cut = [x[k * part : (k + 1) * part] for k in range(len(masks))]
        got = [swap(c, mask, count) for c, mask in zip(cut[1:], masks[1:])]
        x = functools.reduce(jnp.add, got, cut[0])
    parts = [x]
    for bits in reversed(rounds):
        x = parts[0] if len(parts) == 1 else jnp.concatenate(parts)
        parts = [x] + [swap(x, mask, count) for mask in masks_of(bits)[1:]]
    return parts


def solution(mesh):
    sizes = [(axis, mesh.shape[axis]) for axis in AXES]
    count = sizes[0][1] * sizes[1][1]
    rounds = rounds_of(sizes)

    def where(first_scenario):
        scen, wide = [lax.axis_index(axis).astype(jnp.int32) for axis in AXES]
        lead = scen if first_scenario else jnp.int32(1)
        return lead, wide, place_of(scen * sizes[1][1] + wide, rounds)

    def per_device(hess_scen, flags, low_d, low_s, up_d, up_s, coupling, pattern, region, hess_first):
        own, m = hess_first.shape
        rows = packed_rows(m, count)
        factors, keep, send = [], None, None
        for i in range(hess_scen.shape[0]):
            factor, low, high = scenario(
                functools.partial(where, i == 0), region[i : i + 1], hess_scen[i],
                flags[i : i + 1], low_d[i : i + 1], low_s[i : i + 1], up_d[i : i + 1], up_s[i : i + 1],
                coupling[i], pattern[i : i + 1], hess_first, rows, count,
            )
            factors.append(factor)
            keep, send = (low, high) if keep is None else (keep + low, send + high)
        parts = sum_everywhere(keep, send, rounds, count)
        mine = first_section(functools.partial(where, True), parts, own, m, count)
        return (jnp.stack(factors), mine)

    each = P(AXES)
    return jax.shard_map(
        per_device,
        mesh=mesh,
        in_specs=(each,) * 9 + (P("wide", None),),
        out_specs=(each, P("wide", None)),
        check_vma=False,
    )
```

```python
import functools
import jax
import jax.numpy as jnp
from jax import lax
from jax.experimental import pallas as pl
from jax.experimental.pallas import tpu as pltpu
from jax.sharding import PartitionSpec as P

T = 128
Q = 32
F32 = jnp.float32
BF = jnp.bfloat16


def split(x):
    hi = x.astype(BF)
    return hi, (x - hi.astype(F32)).astype(BF)


def dot3(a, b, dims):
    ah, al = a
    bh, bl = b
    d = functools.partial(lax.dot_general, dimension_numbers=(dims, ((), ())), preferred_element_type=F32)
    return d(ah, bh) + (d(ah, bl) + d(al, bh))


NN = ((1,), (0,))
NT = ((1,), (1,))
TN = ((0,), (0,))


def row_splat(v, j):
    return jnp.broadcast_to(v[j : j + 1, :], v.shape)


def lane_splat(v, c):
    return jnp.take_along_axis(v, jnp.full((8, T), c, jnp.int32), axis=1, mode="promise_in_bounds")


def eliminate(rows, lane0):
    sub = lax.broadcasted_iota(jnp.int32, (8, T), 0)
    n = len(rows)
    v = [[r[:, i : i + T] for i in range(0, r.shape[1], T)] for r in rows]
    block = {}

    def fetch(h, k):
        block[h, k] = [lane_splat(v[h][0], lane0 + 8 * k + c) for c in range(8)]

    for h in range(n):
        fetch(h, 0)
    fetch(1, 1)
    out = []
    for g in range(n):
        for h in range(g + 1, n):
            if (h, g) not in block:
                fetch(h, g)
        later = [key for key in block if key[1] > g]
        own = block[g, g]
        pivots = jnp.zeros((8, T), F32)
        pivot = row_splat(own[0], 0)
        for j in range(8):
            pivots = jnp.where(sub == j, pivot, pivots)
            inv = 1.0 / pivot
            if j < 7:
                side = row_splat(own[j], j + 1)
                pivot = row_splat(own[j + 1], j + 1) - (side * side) * inv
            top = [row_splat(w, j) for w in v[g]]
            across = {c: row_splat(own[j], c) for c in range(j + 1, 8)}
            far = {k: [row_splat(block[k, g][j], c) for c in range(8)] for k in sorted({key[1] for key in later})}
            m = {}
            for h in range(g, n):
                here = block[h, g]
                m[h] = here[j] * inv
                for c in range(j + 1, 8):
                    here[c] = here[c] - m[h] * across[c]
            for h, k in later:
                there = block[h, k]
                for c in range(8):
                    there[c] = there[c] - m[h] * far[k][c]
            for h in range(g, n):
                part = jnp.where(sub > j, m[h], 0.0) if h == g else m[h]
                v[h] = [w - part * t for w, t in zip(v[h], top)]
        scale = lax.rsqrt(pivots)
        out.append(jnp.concatenate([w * scale for w in v[g]], axis=1))
        for h in range(g + 2, n):
            for k in (g + 1, g + 2):
                if k <= h and (h, k) not in block:
                    fetch(h, k)
    return out


def factor_block(d_ref):
    for s in range(T // Q):
        rows = [d_ref[pl.ds(Q * s + 8 * h, 8), :] for h in range(Q // 8)]
        done = jnp.concatenate(eliminate(rows, Q * s), axis=0)
        d_ref[pl.ds(Q * s, Q), :] = done
        if s + 1 < T // Q:
            hi, lo = split(done)
            left = jnp.concatenate([hi[:, :T], hi[:, :T], lo[:, :T]], axis=0)
            right = jnp.concatenate([hi, lo, hi], axis=0)
            change = lax.dot_general(left, right, (TN, ((), ())), preferred_element_type=F32)
            below = pl.ds(Q * (s + 1), T - Q * (s + 1))
            d_ref[below, :] = d_ref[below, :] - change[Q * (s + 1) :, :]


def unit_block():
    r = lax.broadcasted_iota(jnp.int32, (T, T), 0)
    c = lax.broadcasted_iota(jnp.int32, (T, T), 1)
    return r, c


def lower_of(d_ref):
    r, c = unit_block()
    return jnp.where(c >= r, d_ref[:, :T], 0.0).T


def scenario_kernel(
    place_fn, count, region, hess_hbm, flags, low_d, low_s, up_d, up_s, coup_hbm, pattern, first,
    factor_hbm, keep, send, hess, coup, factor, d_ref, ih, il, lh, ll, xh, xl, whole, in_sem, out_sem,
):
    n, m = coup.shape
    nt, mt = n // T, m // T
    loads = []
    for k in range(nt):
        cut = (pl.ds(k * T, n - k * T), pl.ds(k * T, T))
        loads.append(pltpu.make_async_copy(hess_hbm.at[cut], hess.at[cut], in_sem.at[k]))
        cut = pl.ds(k * T, T)
        loads.append(pltpu.make_async_copy(coup_hbm.at[cut], coup.at[cut], in_sem.at[nt + k]))
    for load in loads:
        load.start()
    stores = []
    for k in range(nt):
        cut = (slice(None), pl.ds(k * T, T))
        stores.append(pltpu.make_async_copy(factor.at[cut], factor_hbm.at[cut], out_sem.at[k]))
    lead, wide, place = place_fn()
    r, c = unit_block()
    eye = r == c
    barrier = low_d[...] / low_s[...] + flags[...].astype(F32) * up_d[...] / up_s[...]
    nb = pattern.shape[1]
    width = m // nb
    home = (lax.broadcasted_iota(jnp.int32, (1, nb), 1) == region[0]).astype(jnp.int32)
    coupled = jnp.maximum(pattern[...], home).astype(F32)
    block_row = lax.broadcasted_iota(jnp.int32, (nb, m), 0)
    column = lax.broadcasted_iota(jnp.int32, (nb, m), 1)
    spread = jnp.where((column >= block_row * width) & (column < (block_row + 1) * width), 1.0, 0.0)
    mask = jnp.dot(jnp.broadcast_to(coupled, (8, nb)), spread, preferred_element_type=F32)[0:1, :]
    for ref in (lh, ll, xh, xl, ih, il):
        ref[...] = jnp.zeros(ref.shape, BF)

    def solve(t):
        rows = pl.ds(pl.multiple_of(t * T, T), T)
        rhs = coup[rows, :] * mask - dot3((lh[rows, :], ll[rows, :]), (xh[...], xl[...]), NN)
        return rows, dot3((ih[...], il[...]), split(rhs), NN)

    def step(t, _):
        for k in range(nt):

            @pl.when(t == k)
            def _():
                lo, hi = k * T, (k + 1) * T
                loads[2 * k].wait()
                loads[2 * k + 1].wait()
                panel = hess[lo:, lo:hi]
                if k:
                    panel = panel - dot3((lh[lo:, :lo], ll[lo:, :lo]), (lh[lo:hi, :lo], ll[lo:hi, :lo]), NT)
                    factor[:lo, lo:hi] = jnp.zeros((lo, T), F32)
                d_ref[:, :T] = panel[:T] + jnp.where(eye, barrier[:, lo:hi], 0.0)
                d_ref[:, T:] = jnp.where(eye, 1.0, 0.0)
                if k + 1 < nt:
                    factor[hi:, lo:hi] = panel[T:]

        rows, solved = solve(jnp.maximum(t - 1, 0))
        xh[rows, :], xl[rows, :] = split(jnp.where(t > 0, solved, 0.0))
        factor_block(d_ref)
        ih[...], il[...] = split(d_ref[:, T:])
        for k in range(nt):

            @pl.when(t == k)
            def _():
                lo, hi = k * T, (k + 1) * T
                factor[lo:hi, lo:hi] = lower_of(d_ref)
                if k + 1 < nt:
                    below = dot3(split(factor[hi:, lo:hi]), (ih[...], il[...]), NT)
                    factor[hi:, lo:hi] = below
                    lh[hi:, lo:hi], ll[hi:, lo:hi] = split(below)
                stores[k].start()

        return 0

    lax.fori_loop(0, nt, step, 0)
    rows, solved = solve(nt - 1)
    xh[rows, :], xl[rows, :] = split(solved)
    for j in range(0, m, 2 * T):
        a = (xh[:, j:], xl[:, j:])
        b = (xh[:, j : j + 2 * T], xl[:, j : j + 2 * T])
        whole[j:, j : j + 2 * T] = dot3(a, b, TN)

    @pl.when(lead == 0)
    def _():
        own = first.shape[0]
        at = pl.ds(pl.multiple_of(wide * own, 8), own)
        whole[at, :] = whole[at, :] + first[...]

    half = count // 2
    chunk = keep.shape[0] // half
    for side in range(2):

        @pl.when(place // half == side)
        def _():
            for l, at, rows, i, j in pieces(m, count * chunk, count):
                to = pl.multiple_of(((l ^ place) % half) * chunk, 8) + at
                target = (keep, send)[(l // half) ^ side]
                target[pl.ds(to, rows), :] = jnp.zeros((rows, T), F32) if i is None else whole[i : i + rows, j : j + T]

    for store in stores:
        store.wait()


def first_kernel(place_fn, count, *refs):
    _, wide, place = place_fn()
    parts, (out, d_ref, panel_ref, lh, ll, full, packed) = refs[:-7], refs[-7:]
    m = full.shape[0]
    mt = m // T
    r, c = unit_block()
    eye = r == c
    start = [sum(m - i * T for i in range(j)) for j in range(mt)]
    chunk = packed.shape[0] // count
    each = count // len(parts)
    for p in range(count):
        to = pl.multiple_of((place ^ p) * chunk, 8)
        at = (p % each) * chunk
        packed[pl.ds(to, chunk), :] = parts[p // each][at : at + chunk, :]

    def step(t, _):
        for k in range(mt):

            @pl.when(t == k)
            def _():
                lo, hi = k * T, (k + 1) * T
                panel = packed[start[k] : start[k] + m - lo, :]
                if k:
                    panel = panel - dot3((lh[lo:, :lo], ll[lo:, :lo]), (lh[lo:hi, :lo], ll[lo:hi, :lo]), NT)
                d_ref[:, :T] = panel[:T]
                d_ref[:, T:] = jnp.where(eye, 1.0, 0.0)
                if k + 1 < mt:
                    panel_ref[hi:, :] = panel[T:]
                    full[lo:hi, hi:] = jnp.zeros((T, m - hi), F32)

        factor_block(d_ref)
        for k in range(mt):

            @pl.when(t == k)
            def _():
                lo, hi = k * T, (k + 1) * T
                full[lo:hi, lo:hi] = lower_of(d_ref)
                if k + 1 < mt:
                    below = dot3(split(panel_ref[hi:, :]), split(d_ref[:, T:]), NT)
                    full[hi:, lo:hi] = below
                    lh[hi:, lo:hi], ll[hi:, lo:hi] = split(below)

        return 0

    lax.fori_loop(0, mt, step, 0)
    own = out.shape[0]
    out[...] = full[pl.ds(pl.multiple_of(wide * own, 8), own), :]


VMEM = pl.BlockSpec(memory_space=pltpu.VMEM)
SMEM = pl.BlockSpec(memory_space=pltpu.SMEM)
HBM = pl.BlockSpec(memory_space=pltpu.HBM)
GRANT = 24 << 20


def packed_rows(m, devices):
    rows = sum(m - j * T for j in range(m // T))
    unit = 8 * devices
    return -(-rows // unit) * unit


def pieces(m, total, count):
    chunk = total // count
    spans = [(i, j) for j in range(0, m, T) for i in range(j, m, T)]
    cuts = sorted(set(range(0, total, chunk)) | set(range(0, len(spans) * T, T)) | {len(spans) * T, total})
    for lo, hi in zip(cuts, cuts[1:]):
        i, j = spans[lo // T] if lo < len(spans) * T else (None, None)
        yield lo // chunk, lo % chunk, hi - lo, None if i is None else i + lo % T, j


def scenario(place_fn, region, hess, flags, low_d, low_s, up_d, up_s, coup, pattern, first, rows, count):
    n, m = coup.shape
    half = jax.ShapeDtypeStruct((rows // 2, T), F32)
    return pl.pallas_call(
        functools.partial(scenario_kernel, place_fn, count),
        out_shape=(jax.ShapeDtypeStruct((n, n), F32), half, half),
        in_specs=[SMEM, HBM] + [VMEM] * 5 + [HBM, VMEM, VMEM],
        out_specs=(HBM, VMEM, VMEM),
        scratch_shapes=[
            pltpu.VMEM((n, n), F32),
            pltpu.VMEM((n, m), F32),
            pltpu.VMEM((n, n), F32),
            pltpu.VMEM((T, 2 * T), F32),
            pltpu.VMEM((T, T), BF),
            pltpu.VMEM((T, T), BF),
            pltpu.VMEM((n, n), BF),
            pltpu.VMEM((n, n), BF),
            pltpu.VMEM((n, m), BF),
            pltpu.VMEM((n, m), BF),
            pltpu.VMEM((m, m), F32),
            pltpu.SemaphoreType.DMA((2 * n // T,)),
            pltpu.SemaphoreType.DMA((n // T,)),
        ],
        compiler_params=pltpu.CompilerParams(vmem_limit_bytes=GRANT),
        name="scenario",
    )(region, *[pltpu.with_memory_space_constraint(v, pltpu.HBM) for v in (hess, flags, low_d, low_s, up_d, up_s, coup, pattern, first)])


def first_section(place_fn, parts, own, m, count):
    rows = sum(part.shape[0] for part in parts)
    return pl.pallas_call(
        functools.partial(first_kernel, place_fn, count),
        out_shape=jax.ShapeDtypeStruct((own, m), F32),
        in_specs=[VMEM] * len(parts),
        out_specs=VMEM,
        scratch_shapes=[
            pltpu.VMEM((T, 2 * T), F32),
            pltpu.VMEM((m, T), F32),
            pltpu.VMEM((m, m), BF),
            pltpu.VMEM((m, m), BF),
            pltpu.VMEM((m, m), F32),
            pltpu.VMEM((rows, T), F32),
        ],
        compiler_params=pltpu.CompilerParams(vmem_limit_bytes=GRANT),
        name="first_section",
    )(*parts)


AXES = ("scen", "wide")


def swap(x, mask, count):
    return lax.ppermute(x, AXES, [(i, i ^ mask) for i in range(count)])


def rounds_of(sizes):
    (_, scen), (_, wide) = sizes
    bits = [wide << k for k in range(scen.bit_length() - 1)] + [1 << k for k in range(wide.bit_length() - 1)]
    return [bits[:1]] + [bits[k : k + 2] for k in range(1, len(bits), 2)]


def masks_of(bits):
    return [sum(b for k, b in enumerate(bits) if d >> k & 1) for d in range(1 << len(bits))]


def place_of(flat, rounds):
    bits = [bit for group in reversed(rounds) for bit in group]
    return sum(((flat // bit) % 2) << k for k, bit in enumerate(bits))


def farthest_first(n):
    return sorted(range(1, n), key=lambda k: (-k.bit_count(), k))


def sum_everywhere(x, sent, rounds, count):
    x = x + swap(sent, masks_of(rounds[0])[1], count)
    for bits in rounds[1:]:
        masks = masks_of(bits)
        part = x.shape[0] // len(masks)
        cut = [x[k * part : (k + 1) * part] for k in range(len(masks))]
        got = [swap(cut[k], masks[k], count) for k in farthest_first(len(masks))]
        x = functools.reduce(jnp.add, got, cut[0])
    parts = [x]
    for bits in reversed(rounds):
        x = parts[0] if len(parts) == 1 else jnp.concatenate(parts)
        parts = [x] + [swap(x, mask, count) for mask in masks_of(bits)[1:]]
    return parts


def solution(mesh):
    sizes = [(axis, mesh.shape[axis]) for axis in AXES]
    count = sizes[0][1] * sizes[1][1]
    rounds = rounds_of(sizes)

    def where(first_scenario):
        scen, wide = [lax.axis_index(axis).astype(jnp.int32) for axis in AXES]
        lead = scen if first_scenario else jnp.int32(1)
        return lead, wide, place_of(scen * sizes[1][1] + wide, rounds)

    def per_device(hess_scen, flags, low_d, low_s, up_d, up_s, coupling, pattern, region, hess_first):
        own, m = hess_first.shape
        rows = packed_rows(m, count)
        factors, keep, send = [], None, None
        for i in range(hess_scen.shape[0]):
            factor, low, high = scenario(
                functools.partial(where, i == 0), region[i : i + 1], hess_scen[i],
                flags[i : i + 1], low_d[i : i + 1], low_s[i : i + 1], up_d[i : i + 1], up_s[i : i + 1],
                coupling[i], pattern[i : i + 1], hess_first, rows, count,
            )
            factors.append(factor)
            keep, send = (low, high) if keep is None else (keep + low, send + high)
        parts = sum_everywhere(keep, send, rounds, count)
        mine = first_section(functools.partial(where, True), parts, own, m, count)
        return (jnp.stack(factors), mine)

    each = P(AXES)
    return jax.shard_map(
        per_device,
        mesh=mesh,
        in_specs=(each,) * 9 + (P("wide", None),),
        out_specs=(each, P("wide", None)),
        check_vma=False,
    )
```

```python
import functools
import jax
import jax.numpy as jnp
from jax import lax
from jax.experimental import pallas as pl
from jax.experimental.pallas import tpu as pltpu
from jax.sharding import PartitionSpec as P

T = 128
Q = 32
F32 = jnp.float32
BF = jnp.bfloat16


def split(x):
    hi = x.astype(BF)
    return hi, (x - hi.astype(F32)).astype(BF)


def dot3(a, b, dims):
    ah, al = a
    bh, bl = b
    d = functools.partial(lax.dot_general, dimension_numbers=(dims, ((), ())), preferred_element_type=F32)
    return d(ah, bh) + (d(ah, bl) + d(al, bh))


NN = ((1,), (0,))
NT = ((1,), (1,))
TN = ((0,), (0,))


def row_splat(v, j):
    return jnp.broadcast_to(v[j : j + 1, :], v.shape)


def lane_splat(v, c):
    return jnp.take_along_axis(v, jnp.full((8, T), c, jnp.int32), axis=1, mode="promise_in_bounds")


def eliminate(rows, lane0):
    sub = lax.broadcasted_iota(jnp.int32, (8, T), 0)
    n = len(rows)
    v = [[r[:, i : i + T] for i in range(0, r.shape[1], T)] for r in rows]
    block = {}

    def fetch(h, k):
        block[h, k] = [lane_splat(v[h][0], lane0 + 8 * k + c) for c in range(8)]

    for h in range(n):
        fetch(h, 0)
    fetch(1, 1)
    out = []
    for g in range(n):
        for h in range(g + 1, n):
            if (h, g) not in block:
                fetch(h, g)
        later = [key for key in block if key[1] > g]
        own = block[g, g]
        pivots = jnp.zeros((8, T), F32)
        pivot = row_splat(own[0], 0)
        for j in range(8):
            pivots = jnp.where(sub == j, pivot, pivots)
            inv = 1.0 / pivot
            if j < 7:
                side = row_splat(own[j], j + 1)
                pivot = row_splat(own[j + 1], j + 1) - (side * side) * inv
            top = [row_splat(w, j) for w in v[g]]
            across = {c: row_splat(own[j], c) for c in range(j + 1, 8)}
            far = {k: [row_splat(block[k, g][j], c) for c in range(8)] for k in sorted({key[1] for key in later})}
            m = {}
            for h in range(g, n):
                here = block[h, g]
                m[h] = here[j] * inv
                for c in range(j + 1, 8):
                    here[c] = here[c] - m[h] * across[c]
            for h, k in later:
                there = block[h, k]
                for c in range(8):
                    there[c] = there[c] - m[h] * far[k][c]
            for h in range(g, n):
                part = jnp.where(sub > j, m[h], 0.0) if h == g else m[h]
                v[h] = [w - part * t for w, t in zip(v[h], top)]
        scale = lax.rsqrt(pivots)
        out.append(jnp.concatenate([w * scale for w in v[g]], axis=1))
        for h in range(g + 2, n):
            for k in (g + 1, g + 2):
                if k <= h and (h, k) not in block:
                    fetch(h, k)
    return out


def factor_block(d_ref):
    for s in range(T // Q):
        rows = [d_ref[pl.ds(Q * s + 8 * h, 8), :] for h in range(Q // 8)]
        done = jnp.concatenate(eliminate(rows, Q * s), axis=0)
        d_ref[pl.ds(Q * s, Q), :] = done
        if s + 1 < T // Q:
            hi, lo = split(done)
            left = jnp.concatenate([hi[:, :T], hi[:, :T], lo[:, :T]], axis=0)
            right = jnp.concatenate([hi, lo, hi], axis=0)
            change = lax.dot_general(left, right, (TN, ((), ())), preferred_element_type=F32)
            below = pl.ds(Q * (s + 1), T - Q * (s + 1))
            d_ref[below, :] = d_ref[below, :] - change[Q * (s + 1) :, :]


def unit_block():
    r = lax.broadcasted_iota(jnp.int32, (T, T), 0)
    c = lax.broadcasted_iota(jnp.int32, (T, T), 1)
    return r, c


def lower_of(d_ref):
    r, c = unit_block()
    return jnp.where(c >= r, d_ref[:, :T], 0.0).T


def scenario_kernel(
    place_fn, count, region, hess_hbm, flags, low_d, low_s, up_d, up_s, coup_hbm, pattern, first,
    factor_hbm, keep, send, hess, coup, factor, d_ref, ih, il, lh, ll, xh, xl, whole, diagonal, in_sem, out_sem,
):
    n, m = coup.shape
    nt, mt = n // T, m // T
    loads = []
    for k in range(nt):
        cut = (pl.ds(k * T, n - k * T), pl.ds(k * T, T))
        loads.append(pltpu.make_async_copy(hess_hbm.at[cut], hess.at[cut], in_sem.at[k]))
        cut = pl.ds(k * T, T)
        loads.append(pltpu.make_async_copy(coup_hbm.at[cut], coup.at[cut], in_sem.at[nt + k]))
    for load in loads:
        load.start()
    stores = []
    for k in range(nt):
        cut = (slice(None), pl.ds(k * T, T))
        stores.append(pltpu.make_async_copy(factor.at[cut], factor_hbm.at[cut], out_sem.at[k]))
    lead, wide, place = place_fn()
    r, c = unit_block()
    eye = r == c
    barrier = low_d[...] / low_s[...] + flags[...].astype(F32) * up_d[...] / up_s[...]
    nb = pattern.shape[1]
    width = m // nb
    home = (lax.broadcasted_iota(jnp.int32, (1, nb), 1) == region[0]).astype(jnp.int32)
    coupled = jnp.maximum(pattern[...], home).astype(F32)
    block_row = lax.broadcasted_iota(jnp.int32, (nb, m), 0)
    column = lax.broadcasted_iota(jnp.int32, (nb, m), 1)
    spread = jnp.where((column >= block_row * width) & (column < (block_row + 1) * width), 1.0, 0.0)
    mask = jnp.dot(jnp.broadcast_to(coupled, (8, nb)), spread, preferred_element_type=F32)[0:1, :]
    for ref in (lh, ll, xh, xl, ih, il):
        ref[...] = jnp.zeros(ref.shape, BF)

    def solve(t):
        rows = pl.ds(pl.multiple_of(t * T, T), T)
        rhs = coup[rows, :] * mask - dot3((lh[rows, :], ll[rows, :]), (xh[...], xl[...]), NN)
        return rows, dot3((ih[...], il[...]), split(rhs), NN)

    def step(t, _):
        for k in range(nt):

            @pl.when(t == k)
            def _():
                lo, hi = k * T, (k + 1) * T
                loads[2 * k].wait()
                loads[2 * k + 1].wait()
                panel = hess[lo:, lo:hi]
                if k:
                    panel = panel - dot3((lh[lo:, :lo], ll[lo:, :lo]), (lh[lo:hi, :lo], ll[lo:hi, :lo]), NT)
                    factor[:lo, lo:hi] = jnp.zeros((lo, T), F32)
                d_ref[:, :T] = panel[:T] + jnp.where(eye, barrier[:, lo:hi], 0.0)
                d_ref[:, T:] = jnp.where(eye, 1.0, 0.0)
                if k + 1 < nt:
                    factor[hi:, lo:hi] = panel[T:]

        rows, solved = solve(jnp.maximum(t - 1, 0))
        xh[rows, :], xl[rows, :] = split(jnp.where(t > 0, solved, 0.0))
        factor_block(d_ref)
        ih[...], il[...] = split(d_ref[:, T:])
        for k in range(nt):

            @pl.when(t == k)
            def _():
                lo, hi = k * T, (k + 1) * T
                factor[lo:hi, lo:hi] = lower_of(d_ref)
                if k + 1 < nt:
                    below = dot3(split(factor[hi:, lo:hi]), (ih[...], il[...]), NT)
                    factor[hi:, lo:hi] = below
                    lh[hi:, lo:hi], ll[hi:, lo:hi] = split(below)
                stores[k].start()

        return 0

    lax.fori_loop(0, nt, step, 0)
    rows, solved = solve(nt - 1)
    xh[rows, :], xl[rows, :] = split(solved)
    for j in range(0, m, 2 * T):
        a = (xh[:, j:], xl[:, j:])
        b = (xh[:, j : j + 2 * T], xl[:, j : j + 2 * T])
        whole[j:, j : j + 2 * T] = dot3(a, b, TN)

    @pl.when(lead == 0)
    def _():
        own = first.shape[0]
        at = pl.ds(pl.multiple_of(wide * own, 8), own)
        whole[at, :] = whole[at, :] + first[...]

    pack_diagonal(whole, diagonal)
    half = count // 2
    chunk = keep.shape[0] // half
    for side in range(2):

        @pl.when(place // half == side)
        def _():
            for l, at, rows, square, i, j in pieces(m, count * chunk, count):
                to = pl.multiple_of(((l ^ place) % half) * chunk, 8) + at
                target = (keep, send)[(l // half) ^ side]
                source = whole if square else diagonal
                value = jnp.zeros((rows, T), F32) if square is None else source[i : i + rows, j : j + T]
                target[pl.ds(to, rows), :] = value

    for store in stores:
        store.wait()


def first_kernel(place_fn, count, *refs):
    _, wide, place = place_fn()
    parts, (out, d_ref, ahead, lh, ll, full, work, diagonal) = refs[:-8], refs[-8:]
    m = full.shape[0]
    mt = m // T
    r, c = unit_block()
    eye = r == c
    half = count // 2
    chunk = parts[0].shape[0] // half
    for side in range(2):

        @pl.when(place // half == side)
        def _():
            for l, at, rows, square, i, j in pieces(m, count * chunk, count):
                if square is not None:
                    begin = pl.multiple_of(((l ^ place) % half) * chunk, 8) + at
                    target = work if square else diagonal
                    target[i : i + rows, j : j + T] = parts[(l // half) ^ side][pl.ds(begin, rows), :]

    unpack_diagonal(work, diagonal)
    for ref in (lh, ll):
        ref[...] = jnp.zeros(ref.shape, BF)
    ahead[...] = work[:, :T]

    def step(t, _):
        for k in range(mt):

            @pl.when(t == k)
            def _():
                lo, hi = k * T, (k + 1) * T
                panel = ahead[lo:, :]
                if k:
                    last = slice(lo - T, lo)
                    panel = panel - dot3((lh[lo:, last], ll[lo:, last]), (lh[lo:hi, last], ll[lo:hi, last]), NT)
                d_ref[:, :T] = panel[:T]
                d_ref[:, T:] = jnp.where(eye, 1.0, 0.0)
                if k + 1 < mt:
                    full[hi:, lo:hi] = panel[T:]
                    full[lo:hi, hi:] = jnp.zeros((T, m - hi), F32)

        cut = pl.ds(pl.multiple_of(jnp.minimum(t + 1, mt - 1) * T, T), T)
        ahead[...] = work[:, cut] - dot3((lh[...], ll[...]), (lh[cut, :], ll[cut, :]), NT)
        factor_block(d_ref)
        for k in range(mt):

            @pl.when(t == k)
            def _():
                lo, hi = k * T, (k + 1) * T
                full[lo:hi, lo:hi] = lower_of(d_ref)
                if k + 1 < mt:
                    below = dot3(split(full[hi:, lo:hi]), split(d_ref[:, T:]), NT)
                    full[hi:, lo:hi] = below
                    lh[hi:, lo:hi], ll[hi:, lo:hi] = split(below)

        return 0

    lax.fori_loop(0, mt, step, 0)
    own = out.shape[0]
    out[...] = full[pl.ds(pl.multiple_of(wide * own, 8), own), :]


VMEM = pl.BlockSpec(memory_space=pltpu.VMEM)
SMEM = pl.BlockSpec(memory_space=pltpu.SMEM)
HBM = pl.BlockSpec(memory_space=pltpu.HBM)
GRANT = 24 << 20


def spans_of(m):
    mt = m // T
    spans = [(True, i, j, T) for j in range(0, m, T) for i in range(j + T, m, T)]
    if mt % 2:
        spans.append((True, m - T, m - T, T))
    spans.append((False, 0, 0, mt // 2 * 3 * (T // 2)))
    return spans


def packed_rows(m, devices):
    rows = sum(span[3] for span in spans_of(m))
    unit = 8 * devices
    return -(-rows // unit) * unit


def pieces(m, total, count):
    chunk = total // count
    begin = 0
    for square, i, j, rows in spans_of(m):
        lo = begin
        while lo < begin + rows:
            hi = min(begin + rows, (lo // chunk + 1) * chunk)
            yield lo // chunk, lo % chunk, hi - lo, square, i + lo - begin, j
            lo = hi
        begin += rows
    lo = begin
    while lo < total:
        hi = (lo // chunk + 1) * chunk
        yield lo // chunk, lo % chunk, hi - lo, None, None, None
        lo = hi


def left_lanes():
    return lax.broadcasted_iota(jnp.int32, (T // 2, T), 1) < T // 2


def pack_diagonal(square, diagonal):
    h, left = T // 2, left_lanes()
    for p in range(square.shape[0] // (2 * T)):
        a, b = [square[k : k + T, k : k + T] for k in (2 * p * T, (2 * p + 1) * T)]
        at = 3 * h * p
        diagonal[at : at + h, :] = jnp.where(left, a[:h], a[h:])
        diagonal[at + h : at + 2 * h, :] = jnp.where(left, b[:h], b[h:])
        diagonal[at + 2 * h : at + 3 * h, :] = jnp.where(left, a[h:], b[:h])


def unpack_diagonal(square, diagonal):
    h, left = T // 2, left_lanes()
    for p in range(square.shape[0] // (2 * T)):
        at = 3 * h * p
        a, b, side = [diagonal[at + k * h : at + (k + 1) * h, :] for k in range(3)]
        turned = jnp.concatenate([side, side], axis=0).T
        k = 2 * p * T
        square[k : k + h, k : k + T] = jnp.where(left, a, turned[:h])
        square[k + h : k + T, k : k + T] = jnp.where(left, side, a)
        k += T
        square[k : k + h, k : k + T] = jnp.where(left, b, side)
        square[k + h : k + T, k : k + T] = jnp.where(left, turned[h:], b)


def scenario(place_fn, region, hess, flags, low_d, low_s, up_d, up_s, coup, pattern, first, rows, count):
    n, m = coup.shape
    half = jax.ShapeDtypeStruct((rows // 2, T), F32)
    return pl.pallas_call(
        functools.partial(scenario_kernel, place_fn, count),
        out_shape=(jax.ShapeDtypeStruct((n, n), F32), half, half),
        in_specs=[SMEM, HBM] + [VMEM] * 5 + [HBM, VMEM, VMEM],
        out_specs=(HBM, VMEM, VMEM),
        scratch_shapes=[
            pltpu.VMEM((n, n), F32),
            pltpu.VMEM((n, m), F32),
            pltpu.VMEM((n, n), F32),
            pltpu.VMEM((T, 2 * T), F32),
            pltpu.VMEM((T, T), BF),
            pltpu.VMEM((T, T), BF),
            pltpu.VMEM((n, n), BF),
            pltpu.VMEM((n, n), BF),
            pltpu.VMEM((n, m), BF),
            pltpu.VMEM((n, m), BF),
            pltpu.VMEM((m, m), F32),
            pltpu.VMEM((m // (2 * T) * 3 * (T // 2), T), F32),
            pltpu.SemaphoreType.DMA((2 * n // T,)),
            pltpu.SemaphoreType.DMA((n // T,)),
        ],
        compiler_params=pltpu.CompilerParams(vmem_limit_bytes=GRANT),
        name="scenario",
    )(region, *[pltpu.with_memory_space_constraint(v, pltpu.HBM) for v in (hess, flags, low_d, low_s, up_d, up_s, coup, pattern, first)])


def first_section(place_fn, parts, own, m, count):
    return pl.pallas_call(
        functools.partial(first_kernel, place_fn, count),
        out_shape=jax.ShapeDtypeStruct((own, m), F32),
        in_specs=[VMEM] * len(parts),
        out_specs=VMEM,
        scratch_shapes=[
            pltpu.VMEM((T, 2 * T), F32),
            pltpu.VMEM((m, T), F32),
            pltpu.VMEM((m, m), BF),
            pltpu.VMEM((m, m), BF),
            pltpu.VMEM((m, m), F32),
            pltpu.VMEM((m, m), F32),
            pltpu.VMEM((m // (2 * T) * 3 * (T // 2), T), F32),
        ],
        compiler_params=pltpu.CompilerParams(vmem_limit_bytes=GRANT),
        name="first_section",
    )(*parts)


AXES = ("scen", "wide")


def swap(x, mask, count):
    return lax.ppermute(x, AXES, [(i, i ^ mask) for i in range(count)])


def rounds_of(sizes):
    (_, scen), (_, wide) = sizes
    bits = [wide << k for k in range(scen.bit_length() - 1)] + [1 << k for k in range(wide.bit_length() - 1)]
    return [bits[:1]] + [bits[k : k + 2] for k in range(1, len(bits), 2)]


def masks_of(bits):
    return [sum(b for k, b in enumerate(bits) if d >> k & 1) for d in range(1 << len(bits))]


def place_of(flat, rounds):
    bits = [bit for group in reversed(rounds) for bit in group]
    return sum(((flat // bit) % 2) << k for k, bit in enumerate(bits))


def farthest_first(n):
    return sorted(range(1, n), key=lambda k: (-k.bit_count(), k))


def sum_everywhere(x, sent, rounds, count):
    x = x + swap(sent, masks_of(rounds[0])[1], count)
    for bits in rounds[1:]:
        masks = masks_of(bits)
        part = x.shape[0] // len(masks)
        cut = [x[k * part : (k + 1) * part] for k in range(len(masks))]
        got = [swap(cut[k], masks[k], count) for k in farthest_first(len(masks))]
        x = functools.reduce(jnp.add, got, cut[0])
    parts = [x]
    for bits in reversed(rounds):
        x = parts[0] if len(parts) == 1 else jnp.concatenate(parts)
        parts = [x] + [swap(x, mask, count) for mask in masks_of(bits)[1:]]
    return parts


def solution(mesh):
    sizes = [(axis, mesh.shape[axis]) for axis in AXES]
    count = sizes[0][1] * sizes[1][1]
    rounds = rounds_of(sizes)

    def where(first_scenario):
        scen, wide = [lax.axis_index(axis).astype(jnp.int32) for axis in AXES]
        lead = scen if first_scenario else jnp.int32(1)
        return lead, wide, place_of(scen * sizes[1][1] + wide, rounds)

    def per_device(hess_scen, flags, low_d, low_s, up_d, up_s, coupling, pattern, region, hess_first):
        own, m = hess_first.shape
        rows = packed_rows(m, count)
        factors, keep, send = [], None, None
        for i in range(hess_scen.shape[0]):
            factor, low, high = scenario(
                functools.partial(where, i == 0), region[i : i + 1], hess_scen[i],
                flags[i : i + 1], low_d[i : i + 1], low_s[i : i + 1], up_d[i : i + 1], up_s[i : i + 1],
                coupling[i], pattern[i : i + 1], hess_first, rows, count,
            )
            factors.append(factor)
            keep, send = (low, high) if keep is None else (keep + low, send + high)
        parts = sum_everywhere(keep, send, rounds, count)
        mine = first_section(functools.partial(where, True), parts, own, m, count)
        return (jnp.stack(factors), mine)

    each = P(AXES)
    return jax.shard_map(
        per_device,
        mesh=mesh,
        in_specs=(each,) * 9 + (P("wide", None),),
        out_specs=(each, P("wide", None)),
        check_vma=False,
    )
```

```python
import functools
import jax
import jax.numpy as jnp
from jax import lax
from jax.experimental import pallas as pl
from jax.experimental.pallas import tpu as pltpu
from jax.sharding import PartitionSpec as P

T = 128
Q = 32
F32 = jnp.float32
BF = jnp.bfloat16


def split(x):
    hi = x.astype(BF)
    return hi, (x - hi.astype(F32)).astype(BF)


def dot3(a, b, dims):
    ah, al = a
    bh, bl = b
    d = functools.partial(lax.dot_general, dimension_numbers=(dims, ((), ())), preferred_element_type=F32)
    return d(ah, bh) + (d(ah, bl) + d(al, bh))


NN = ((1,), (0,))
NT = ((1,), (1,))
TN = ((0,), (0,))


def row_splat(v, j):
    return jnp.broadcast_to(v[j : j + 1, :], v.shape)


def lane_splat(v, c):
    return jnp.take_along_axis(v, jnp.full((8, T), c, jnp.int32), axis=1, mode="promise_in_bounds")


def eliminate(rows, lane0):
    sub = lax.broadcasted_iota(jnp.int32, (8, T), 0)
    n = len(rows)
    v = [[r[:, i : i + T] for i in range(0, r.shape[1], T)] for r in rows]
    block = {}

    def fetch(h, k):
        block[h, k] = [lane_splat(v[h][0], lane0 + 8 * k + c) for c in range(8)]

    for h in range(n):
        fetch(h, 0)
    fetch(1, 1)
    out = []
    for g in range(n):
        for h in range(g + 1, n):
            if (h, g) not in block:
                fetch(h, g)
        later = [key for key in block if key[1] > g]
        own = block[g, g]
        pivots = jnp.zeros((8, T), F32)
        pivot = row_splat(own[0], 0)
        for j in range(8):
            pivots = jnp.where(sub == j, pivot, pivots)
            inv = 1.0 / pivot
            if j < 7:
                side = row_splat(own[j], j + 1)
                pivot = row_splat(own[j + 1], j + 1) - (side * side) * inv
            top = [row_splat(w, j) for w in v[g]]
            across = {c: row_splat(own[j], c) for c in range(j + 1, 8)}
            far = {k: [row_splat(block[k, g][j], c) for c in range(8)] for k in sorted({key[1] for key in later})}
            m = {}
            for h in range(g, n):
                here = block[h, g]
                m[h] = here[j] * inv
                for c in range(j + 1, 8):
                    here[c] = here[c] - m[h] * across[c]
            for h, k in later:
                there = block[h, k]
                for c in range(8):
                    there[c] = there[c] - m[h] * far[k][c]
            for h in range(g, n):
                part = jnp.where(sub > j, m[h], 0.0) if h == g else m[h]
                v[h] = [w - part * t for w, t in zip(v[h], top)]
        scale = lax.rsqrt(pivots)
        out.append(jnp.concatenate([w * scale for w in v[g]], axis=1))
        for h in range(g + 2, n):
            for k in (g + 1, g + 2):
                if k <= h and (h, k) not in block:
                    fetch(h, k)
    return out


def factor_block(d_ref):
    for s in range(T // Q):
        rows = [d_ref[pl.ds(Q * s + 8 * h, 8), :] for h in range(Q // 8)]
        done = jnp.concatenate(eliminate(rows, Q * s), axis=0)
        d_ref[pl.ds(Q * s, Q), :] = done
        if s + 1 < T // Q:
            hi, lo = split(done)
            left = jnp.concatenate([hi[:, :T], hi[:, :T], lo[:, :T]], axis=0)
            right = jnp.concatenate([hi, lo, hi], axis=0)
            change = lax.dot_general(left, right, (TN, ((), ())), preferred_element_type=F32)
            below = pl.ds(Q * (s + 1), T - Q * (s + 1))
            d_ref[below, :] = d_ref[below, :] - change[Q * (s + 1) :, :]


def unit_block():
    r = lax.broadcasted_iota(jnp.int32, (T, T), 0)
    c = lax.broadcasted_iota(jnp.int32, (T, T), 1)
    return r, c


def lower_of(d_ref):
    r, c = unit_block()
    return jnp.where(c >= r, d_ref[:, :T], 0.0).T


def scenario_kernel(
    place_fn, count, region, hess_hbm, flags, low_d, low_s, up_d, up_s, coup_hbm, pattern, first,
    factor_hbm, keep, send, hess, coup, factor, d_ref, ih, il, lh, ll, xh, xl, whole, diagonal, in_sem, out_sem,
):
    n, m = coup.shape
    nt, mt = n // T, m // T
    loads = []
    for k in range(nt):
        cut = (pl.ds(k * T, n - k * T), pl.ds(k * T, T))
        loads.append(pltpu.make_async_copy(hess_hbm.at[cut], hess.at[cut], in_sem.at[k]))
        cut = pl.ds(k * T, T)
        loads.append(pltpu.make_async_copy(coup_hbm.at[cut], coup.at[cut], in_sem.at[nt + k]))
    for load in loads:
        load.start()
    stores = []
    for k in range(nt):
        cut = (slice(None), pl.ds(k * T, T))
        stores.append(pltpu.make_async_copy(factor.at[cut], factor_hbm.at[cut], out_sem.at[k]))
    lead, wide, place = place_fn()
    r, c = unit_block()
    eye = r == c
    barrier = low_d[...] / low_s[...] + flags[...].astype(F32) * up_d[...] / up_s[...]
    nb = pattern.shape[1]
    width = m // nb
    home = (lax.broadcasted_iota(jnp.int32, (1, nb), 1) == region[0]).astype(jnp.int32)
    coupled = jnp.maximum(pattern[...], home).astype(F32)
    block_row = lax.broadcasted_iota(jnp.int32, (nb, m), 0)
    column = lax.broadcasted_iota(jnp.int32, (nb, m), 1)
    spread = jnp.where((column >= block_row * width) & (column < (block_row + 1) * width), 1.0, 0.0)
    mask = jnp.dot(jnp.broadcast_to(coupled, (8, nb)), spread, preferred_element_type=F32)[0:1, :]
    for ref in (lh, ll, xh, xl, ih, il):
        ref[...] = jnp.zeros(ref.shape, BF)

    def solve(t):
        rows = pl.ds(pl.multiple_of(t * T, T), T)
        rhs = coup[rows, :] * mask - dot3((lh[rows, :], ll[rows, :]), (xh[...], xl[...]), NN)
        return rows, dot3((ih[...], il[...]), split(rhs), NN)

    def step(t, _):
        for k in range(nt):

            @pl.when(t == k)
            def _():
                lo, hi = k * T, (k + 1) * T
                loads[2 * k].wait()
                loads[2 * k + 1].wait()
                panel = hess[lo:, lo:hi]
                if k:
                    panel = panel - dot3((lh[lo:, :lo], ll[lo:, :lo]), (lh[lo:hi, :lo], ll[lo:hi, :lo]), NT)
                    factor[:lo, lo:hi] = jnp.zeros((lo, T), F32)
                d_ref[:, :T] = panel[:T] + jnp.where(eye, barrier[:, lo:hi], 0.0)
                d_ref[:, T:] = jnp.where(eye, 1.0, 0.0)
                if k + 1 < nt:
                    factor[hi:, lo:hi] = panel[T:]

        rows, solved = solve(jnp.maximum(t - 1, 0))
        xh[rows, :], xl[rows, :] = split(jnp.where(t > 0, solved, 0.0))
        factor_block(d_ref)
        ih[...], il[...] = split(d_ref[:, T:])
        for k in range(nt):

            @pl.when(t == k)
            def _():
                lo, hi = k * T, (k + 1) * T
                factor[lo:hi, lo:hi] = lower_of(d_ref)
                if k + 1 < nt:
                    below = dot3(split(factor[hi:, lo:hi]), (ih[...], il[...]), NT)
                    factor[hi:, lo:hi] = below
                    lh[hi:, lo:hi], ll[hi:, lo:hi] = split(below)
                stores[k].start()

        return 0

    lax.fori_loop(0, nt, step, 0)
    rows, solved = solve(nt - 1)
    xh[rows, :], xl[rows, :] = split(solved)
    for j in range(0, m, 2 * T):
        a = (xh[:, j:], xl[:, j:])
        b = (xh[:, j : j + 2 * T], xl[:, j : j + 2 * T])
        whole[j:, j : j + 2 * T] = dot3(a, b, TN)

    @pl.when(lead == 0)
    def _():
        own = first.shape[0]
        at = pl.ds(pl.multiple_of(wide * own, 8), own)
        whole[at, :] = whole[at, :] + first[...]

    pack_diagonal(whole, diagonal)
    half = count // 2
    chunk = keep.shape[0] // half
    for side in range(2):

        @pl.when(place // half == side)
        def _():
            for l, at, rows, square, i, j in pieces(m, count * chunk, count):
                to = pl.multiple_of(((l ^ place) % half) * chunk, 8) + at
                target = (keep, send)[(l // half) ^ side]
                source = whole if square else diagonal
                value = jnp.zeros((rows, T), F32) if square is None else source[i : i + rows, j : j + T]
                target[pl.ds(to, rows), :] = value

    for store in stores:
        store.wait()


def first_kernel(place_fn, count, *refs):
    _, wide, place = place_fn()
    parts, (out, d_ref, lh, ll, full, work, diagonal) = refs[:-7], refs[-7:]
    m = full.shape[0]
    mt = m // T
    r, c = unit_block()
    eye = r == c
    half = count // 2
    chunk = parts[0].shape[0] // half
    for side in range(2):

        @pl.when(place // half == side)
        def _():
            for l, at, rows, square, i, j in pieces(m, count * chunk, count):
                if square is not None:
                    begin = pl.multiple_of(((l ^ place) % half) * chunk, 8) + at
                    target = work if square else diagonal
                    target[i : i + rows, j : j + T] = parts[(l // half) ^ side][pl.ds(begin, rows), :]

    unpack_diagonal(work, diagonal)

    def step(t, _):
        for k in range(mt):

            @pl.when(t == k)
            def _():
                lo, hi = k * T, (k + 1) * T
                panel = work[lo:, lo:hi]
                if k:
                    panel = panel - dot3((lh[lo:, :lo], ll[lo:, :lo]), (lh[lo:hi, :lo], ll[lo:hi, :lo]), NT)
                d_ref[:, :T] = panel[:T]
                d_ref[:, T:] = jnp.where(eye, 1.0, 0.0)
                if k + 1 < mt:
                    full[hi:, lo:hi] = panel[T:]
                    full[lo:hi, hi:] = jnp.zeros((T, m - hi), F32)

        factor_block(d_ref)
        for k in range(mt):

            @pl.when(t == k)
            def _():
                lo, hi = k * T, (k + 1) * T
                full[lo:hi, lo:hi] = lower_of(d_ref)
                if k + 1 < mt:
                    below = dot3(split(full[hi:, lo:hi]), split(d_ref[:, T:]), NT)
                    full[hi:, lo:hi] = below
                    lh[hi:, lo:hi], ll[hi:, lo:hi] = split(below)

        return 0

    lax.fori_loop(0, mt, step, 0)
    own = out.shape[0]
    out[...] = full[pl.ds(pl.multiple_of(wide * own, 8), own), :]


VMEM = pl.BlockSpec(memory_space=pltpu.VMEM)
SMEM = pl.BlockSpec(memory_space=pltpu.SMEM)
HBM = pl.BlockSpec(memory_space=pltpu.HBM)
GRANT = 24 << 20


def spans_of(m):
    mt = m // T
    spans = [(True, i, j, T) for j in range(0, m, T) for i in range(j + T, m, T)]
    if mt % 2:
        spans.append((True, m - T, m - T, T))
    spans.append((False, 0, 0, mt // 2 * 3 * (T // 2)))
    return spans


def packed_rows(m, devices):
    rows = sum(span[3] for span in spans_of(m))
    unit = 8 * devices
    return -(-rows // unit) * unit


def pieces(m, total, count):
    chunk = total // count
    begin = 0
    for square, i, j, rows in spans_of(m):
        lo = begin
        while lo < begin + rows:
            hi = min(begin + rows, (lo // chunk + 1) * chunk)
            yield lo // chunk, lo % chunk, hi - lo, square, i + lo - begin, j
            lo = hi
        begin += rows
    lo = begin
    while lo < total:
        hi = (lo // chunk + 1) * chunk
        yield lo // chunk, lo % chunk, hi - lo, None, None, None
        lo = hi


def left_lanes():
    return lax.broadcasted_iota(jnp.int32, (T // 2, T), 1) < T // 2


def pack_diagonal(square, diagonal):
    h, left = T // 2, left_lanes()
    for p in range(square.shape[0] // (2 * T)):
        a, b = [square[k : k + T, k : k + T] for k in (2 * p * T, (2 * p + 1) * T)]
        at = 3 * h * p
        diagonal[at : at + h, :] = jnp.where(left, a[:h], a[h:])
        diagonal[at + h : at + 2 * h, :] = jnp.where(left, b[:h], b[h:])
        diagonal[at + 2 * h : at + 3 * h, :] = jnp.where(left, a[h:], b[:h])


def unpack_diagonal(square, diagonal):
    h, left = T // 2, left_lanes()
    for p in range(square.shape[0] // (2 * T)):
        at = 3 * h * p
        a, b, side = [diagonal[at + k * h : at + (k + 1) * h, :] for k in range(3)]
        turned = jnp.concatenate([side, side], axis=0).T
        k = 2 * p * T
        square[k : k + h, k : k + T] = jnp.where(left, a, turned[:h])
        square[k + h : k + T, k : k + T] = jnp.where(left, side, a)
        k += T
        square[k : k + h, k : k + T] = jnp.where(left, b, side)
        square[k + h : k + T, k : k + T] = jnp.where(left, turned[h:], b)


def scenario(place_fn, region, hess, flags, low_d, low_s, up_d, up_s, coup, pattern, first, rows, count):
    n, m = coup.shape
    half = jax.ShapeDtypeStruct((rows // 2, T), F32)
    return pl.pallas_call(
        functools.partial(scenario_kernel, place_fn, count),
        out_shape=(jax.ShapeDtypeStruct((n, n), F32), half, half),
        in_specs=[SMEM, HBM] + [VMEM] * 5 + [HBM, VMEM, VMEM],
        out_specs=(HBM, VMEM, VMEM),
        scratch_shapes=[
            pltpu.VMEM((n, n), F32),
            pltpu.VMEM((n, m), F32),
            pltpu.VMEM((n, n), F32),
            pltpu.VMEM((T, 2 * T), F32),
            pltpu.VMEM((T, T), BF),
            pltpu.VMEM((T, T), BF),
            pltpu.VMEM((n, n), BF),
            pltpu.VMEM((n, n), BF),
            pltpu.VMEM((n, m), BF),
            pltpu.VMEM((n, m), BF),
            pltpu.VMEM((m, m), F32),
            pltpu.VMEM((m // (2 * T) * 3 * (T // 2), T), F32),
            pltpu.SemaphoreType.DMA((2 * n // T,)),
            pltpu.SemaphoreType.DMA((n // T,)),
        ],
        compiler_params=pltpu.CompilerParams(vmem_limit_bytes=GRANT),
        name="scenario",
    )(region, *[pltpu.with_memory_space_constraint(v, pltpu.HBM) for v in (hess, flags, low_d, low_s, up_d, up_s, coup, pattern, first)])


def first_section(place_fn, parts, own, m, count):
    return pl.pallas_call(
        functools.partial(first_kernel, place_fn, count),
        out_shape=jax.ShapeDtypeStruct((own, m), F32),
        in_specs=[VMEM] * len(parts),
        out_specs=VMEM,
        scratch_shapes=[
            pltpu.VMEM((T, 2 * T), F32),
            pltpu.VMEM((m, m), BF),
            pltpu.VMEM((m, m), BF),
            pltpu.VMEM((m, m), F32),
            pltpu.VMEM((m, m), F32),
            pltpu.VMEM((m // (2 * T) * 3 * (T // 2), T), F32),
        ],
        compiler_params=pltpu.CompilerParams(vmem_limit_bytes=GRANT),
        name="first_section",
    )(*parts)


AXES = ("scen", "wide")


def swap(x, mask, count):
    return lax.ppermute(x, AXES, [(i, i ^ mask) for i in range(count)])


def rounds_of(sizes):
    (_, scen), (_, wide) = sizes
    bits = [wide << k for k in range(scen.bit_length() - 1)] + [1 << k for k in range(wide.bit_length() - 1)]
    return [bits[:1]] + [bits[k : k + 2] for k in range(1, len(bits), 2)]


def masks_of(bits):
    return [sum(b for k, b in enumerate(bits) if d >> k & 1) for d in range(1 << len(bits))]


def place_of(flat, rounds):
    bits = [bit for group in reversed(rounds) for bit in group]
    return sum(((flat // bit) % 2) << k for k, bit in enumerate(bits))


def farthest_first(n):
    return sorted(range(1, n), key=lambda k: (-k.bit_count(), k))


def sum_everywhere(x, sent, rounds, count):
    x = x + swap(sent, masks_of(rounds[0])[1], count)
    for bits in rounds[1:]:
        masks = masks_of(bits)
        part = x.shape[0] // len(masks)
        cut = [x[k * part : (k + 1) * part] for k in range(len(masks))]
        got = [swap(cut[k], masks[k], count) for k in farthest_first(len(masks))]
        x = functools.reduce(jnp.add, got, cut[0])
    parts = [x]
    for bits in reversed(rounds):
        x = parts[0] if len(parts) == 1 else jnp.concatenate(parts)
        parts = [x] + [swap(x, mask, count) for mask in masks_of(bits)[1:]]
    return parts


def solution(mesh):
    sizes = [(axis, mesh.shape[axis]) for axis in AXES]
    count = sizes[0][1] * sizes[1][1]
    rounds = rounds_of(sizes)

    def where(first_scenario):
        scen, wide = [lax.axis_index(axis).astype(jnp.int32) for axis in AXES]
        lead = scen if first_scenario else jnp.int32(1)
        return lead, wide, place_of(scen * sizes[1][1] + wide, rounds)

    def per_device(hess_scen, flags, low_d, low_s, up_d, up_s, coupling, pattern, region, hess_first):
        own, m = hess_first.shape
        rows = packed_rows(m, count)
        factors, keep, send = [], None, None
        for i in range(hess_scen.shape[0]):
            factor, low, high = scenario(
                functools.partial(where, i == 0), region[i : i + 1], hess_scen[i],
                flags[i : i + 1], low_d[i : i + 1], low_s[i : i + 1], up_d[i : i + 1], up_s[i : i + 1],
                coupling[i], pattern[i : i + 1], hess_first, rows, count,
            )
            factors.append(factor)
            keep, send = (low, high) if keep is None else (keep + low, send + high)
        parts = sum_everywhere(keep, send, rounds, count)
        mine = first_section(functools.partial(where, True), parts, own, m, count)
        return (jnp.stack(factors), mine)

    each = P(AXES)
    return jax.shard_map(
        per_device,
        mesh=mesh,
        in_specs=(each,) * 9 + (P("wide", None),),
        out_specs=(each, P("wide", None)),
        check_vma=False,
    )
```

```python
import functools
import jax
import jax.numpy as jnp
from jax import lax
from jax.experimental import pallas as pl
from jax.experimental.pallas import tpu as pltpu
from jax.sharding import PartitionSpec as P

T = 128
Q = 32
F32 = jnp.float32
BF = jnp.bfloat16


def split(x):
    hi = x.astype(BF)
    return hi, (x - hi.astype(F32)).astype(BF)


def dot3(a, b, dims):
    ah, al = a
    bh, bl = b
    d = functools.partial(lax.dot_general, dimension_numbers=(dims, ((), ())), preferred_element_type=F32)
    return d(ah, bh) + (d(ah, bl) + d(al, bh))


NN = ((1,), (0,))
NT = ((1,), (1,))
TN = ((0,), (0,))


def row_splat(v, j):
    return jnp.broadcast_to(v[j : j + 1, :], v.shape)


def lane_splat(v, c):
    return jnp.take_along_axis(v, jnp.full((8, T), c, jnp.int32), axis=1, mode="promise_in_bounds")


def eliminate(rows, lane0):
    sub = lax.broadcasted_iota(jnp.int32, (8, T), 0)
    n = len(rows)
    v = [[r[:, i : i + T] for i in range(0, r.shape[1], T)] for r in rows]
    block = {}

    def fetch(h, k):
        block[h, k] = [lane_splat(v[h][0], lane0 + 8 * k + c) for c in range(8)]

    for h in range(n):
        fetch(h, 0)
    fetch(1, 1)
    out = []
    for g in range(n):
        for h in range(g + 1, n):
            if (h, g) not in block:
                fetch(h, g)
        later = [key for key in block if key[1] > g]
        own = block[g, g]
        pivots = jnp.zeros((8, T), F32)
        pivot = row_splat(own[0], 0)
        for j in range(8):
            pivots = jnp.where(sub == j, pivot, pivots)
            inv = 1.0 / pivot
            if j < 7:
                side = row_splat(own[j], j + 1)
                pivot = row_splat(own[j + 1], j + 1) - (side * side) * inv
            top = [row_splat(w, j) for w in v[g]]
            across = {c: row_splat(own[j], c) for c in range(j + 1, 8)}
            far = {k: [row_splat(block[k, g][j], c) for c in range(8)] for k in sorted({key[1] for key in later})}
            m = {}
            for h in range(g, n):
                here = block[h, g]
                m[h] = here[j] * inv
                for c in range(j + 1, 8):
                    here[c] = here[c] - m[h] * across[c]
            for h, k in later:
                there = block[h, k]
                for c in range(8):
                    there[c] = there[c] - m[h] * far[k][c]
            for h in range(g, n):
                part = jnp.where(sub > j, m[h], 0.0) if h == g else m[h]
                v[h] = [w - part * t for w, t in zip(v[h], top)]
        scale = lax.rsqrt(pivots)
        out.append(jnp.concatenate([w * scale for w in v[g]], axis=1))
        for h in range(g + 2, n):
            for k in (g + 1, g + 2):
                if k <= h and (h, k) not in block and (k == g + 1 or h == k):
                    fetch(h, k)
    return out


def factor_block(d_ref):
    for s in range(T // Q):
        rows = [d_ref[pl.ds(Q * s + 8 * h, 8), :] for h in range(Q // 8)]
        done = jnp.concatenate(eliminate(rows, Q * s), axis=0)
        d_ref[pl.ds(Q * s, Q), :] = done
        if s + 1 < T // Q:
            hi, lo = split(done)
            left = jnp.concatenate([hi[:, :T], hi[:, :T], lo[:, :T]], axis=0)
            right = jnp.concatenate([hi, lo, hi], axis=0)
            change = lax.dot_general(left, right, (TN, ((), ())), preferred_element_type=F32)
            below = pl.ds(Q * (s + 1), T - Q * (s + 1))
            d_ref[below, :] = d_ref[below, :] - change[Q * (s + 1) :, :]


def unit_block():
    r = lax.broadcasted_iota(jnp.int32, (T, T), 0)
    c = lax.broadcasted_iota(jnp.int32, (T, T), 1)
    return r, c


def lower_of(d_ref):
    r, c = unit_block()
    return jnp.where(c >= r, d_ref[:, :T], 0.0).T


def scenario_kernel(
    place_fn, count, region, hess_hbm, flags, low_d, low_s, up_d, up_s, coup_hbm, pattern, first,
    factor_hbm, keep, send, hess, coup, factor, d_ref, ih, il, lh, ll, xh, xl, whole, diagonal, in_sem, out_sem,
):
    n, m = coup.shape
    nt, mt = n // T, m // T
    loads = []
    for k in range(nt):
        cut = (pl.ds(k * T, n - k * T), pl.ds(k * T, T))
        loads.append(pltpu.make_async_copy(hess_hbm.at[cut], hess.at[cut], in_sem.at[k]))
        cut = pl.ds(k * T, T)
        loads.append(pltpu.make_async_copy(coup_hbm.at[cut], coup.at[cut], in_sem.at[nt + k]))
    for load in loads:
        load.start()
    stores = []
    for k in range(nt):
        cut = (slice(None), pl.ds(k * T, T))
        stores.append(pltpu.make_async_copy(factor.at[cut], factor_hbm.at[cut], out_sem.at[k]))
    lead, wide, place = place_fn()
    r, c = unit_block()
    eye = r == c
    barrier = low_d[...] / low_s[...] + flags[...].astype(F32) * up_d[...] / up_s[...]
    nb = pattern.shape[1]
    width = m // nb
    home = (lax.broadcasted_iota(jnp.int32, (1, nb), 1) == region[0]).astype(jnp.int32)
    coupled = jnp.maximum(pattern[...], home).astype(F32)
    block_row = lax.broadcasted_iota(jnp.int32, (nb, m), 0)
    column = lax.broadcasted_iota(jnp.int32, (nb, m), 1)
    spread = jnp.where((column >= block_row * width) & (column < (block_row + 1) * width), 1.0, 0.0)
    mask = jnp.dot(jnp.broadcast_to(coupled, (8, nb)), spread, preferred_element_type=F32)[0:1, :]
    for ref in (lh, ll, xh, xl, ih, il):
        ref[...] = jnp.zeros(ref.shape, BF)

    def solve(t):
        rows = pl.ds(pl.multiple_of(t * T, T), T)
        rhs = coup[rows, :] * mask - dot3((lh[rows, :], ll[rows, :]), (xh[...], xl[...]), NN)
        return rows, dot3((ih[...], il[...]), split(rhs), NN)

    def step(t, _):
        for k in range(nt):

            @pl.when(t == k)
            def _():
                lo, hi = k * T, (k + 1) * T
                loads[2 * k].wait()
                loads[2 * k + 1].wait()
                panel = hess[lo:, lo:hi]
                if k:
                    panel = panel - dot3((lh[lo:, :lo], ll[lo:, :lo]), (lh[lo:hi, :lo], ll[lo:hi, :lo]), NT)
                    factor[:lo, lo:hi] = jnp.zeros((lo, T), F32)
                d_ref[:, :T] = panel[:T] + jnp.where(eye, barrier[:, lo:hi], 0.0)
                d_ref[:, T:] = jnp.where(eye, 1.0, 0.0)
                if k + 1 < nt:
                    factor[hi:, lo:hi] = panel[T:]

        rows, solved = solve(jnp.maximum(t - 1, 0))
        xh[rows, :], xl[rows, :] = split(jnp.where(t > 0, solved, 0.0))
        factor_block(d_ref)
        ih[...], il[...] = split(d_ref[:, T:])
        for k in range(nt):

            @pl.when(t == k)
            def _():
                lo, hi = k * T, (k + 1) * T
                factor[lo:hi, lo:hi] = lower_of(d_ref)
                if k + 1 < nt:
                    below = dot3(split(factor[hi:, lo:hi]), (ih[...], il[...]), NT)
                    factor[hi:, lo:hi] = below
                    lh[hi:, lo:hi], ll[hi:, lo:hi] = split(below)
                stores[k].start()

        return 0

    lax.fori_loop(0, nt, step, 0)
    rows, solved = solve(nt - 1)
    xh[rows, :], xl[rows, :] = split(solved)
    for j in range(0, m, 2 * T):
        a = (xh[:, j:], xl[:, j:])
        b = (xh[:, j : j + 2 * T], xl[:, j : j + 2 * T])
        whole[j:, j : j + 2 * T] = dot3(a, b, TN)

    @pl.when(lead == 0)
    def _():
        own = first.shape[0]
        at = pl.ds(pl.multiple_of(wide * own, 8), own)
        whole[at, :] = whole[at, :] + first[...]

    pack_diagonal(whole, diagonal)
    half = count // 2
    chunk = keep.shape[0] // half
    for side in range(2):

        @pl.when(place // half == side)
        def _():
            for l, at, rows, square, i, j in pieces(m, count * chunk, count):
                to = pl.multiple_of(((l ^ place) % half) * chunk, 8) + at
                target = (keep, send)[(l // half) ^ side]
                source = whole if square else diagonal
                value = jnp.zeros((rows, T), F32) if square is None else source[i : i + rows, j : j + T]
                target[pl.ds(to, rows), :] = value

    for store in stores:
        store.wait()


def first_kernel(place_fn, count, *refs):
    _, wide, place = place_fn()
    parts, (out, d_ref, lh, ll, full, work, diagonal) = refs[:-7], refs[-7:]
    m = full.shape[0]
    mt = m // T
    r, c = unit_block()
    eye = r == c
    each = count // len(parts)
    chunk = parts[0].shape[0] // each
    for top in range(len(parts)):

        @pl.when(place // each == top)
        def _():
            for l, at, rows, square, i, j in pieces(m, count * chunk, count):
                if square is not None:
                    begin = pl.multiple_of(((l ^ place) % each) * chunk, 8) + at
                    target = work if square else diagonal
                    target[i : i + rows, j : j + T] = parts[(l // each) ^ top][pl.ds(begin, rows), :]

    unpack_diagonal(work, diagonal)

    def step(t, _):
        for k in range(mt):

            @pl.when(t == k)
            def _():
                lo, hi = k * T, (k + 1) * T
                panel = work[lo:, lo:hi]
                if k:
                    panel = panel - dot3((lh[lo:, :lo], ll[lo:, :lo]), (lh[lo:hi, :lo], ll[lo:hi, :lo]), NT)
                d_ref[:, :T] = panel[:T]
                d_ref[:, T:] = jnp.where(eye, 1.0, 0.0)
                if k + 1 < mt:
                    full[hi:, lo:hi] = panel[T:]
                    full[lo:hi, hi:] = jnp.zeros((T, m - hi), F32)

        factor_block(d_ref)
        for k in range(mt):

            @pl.when(t == k)
            def _():
                lo, hi = k * T, (k + 1) * T
                full[lo:hi, lo:hi] = lower_of(d_ref)
                if k + 1 < mt:
                    below = dot3(split(full[hi:, lo:hi]), split(d_ref[:, T:]), NT)
                    full[hi:, lo:hi] = below
                    lh[hi:, lo:hi], ll[hi:, lo:hi] = split(below)

        return 0

    lax.fori_loop(0, mt, step, 0)
    own = out.shape[0]
    out[...] = full[pl.ds(pl.multiple_of(wide * own, 8), own), :]


VMEM = pl.BlockSpec(memory_space=pltpu.VMEM)
SMEM = pl.BlockSpec(memory_space=pltpu.SMEM)
HBM = pl.BlockSpec(memory_space=pltpu.HBM)
GRANT = 24 << 20


def spans_of(m):
    mt = m // T
    spans = [(True, i, j, T) for j in range(0, m, T) for i in range(j + T, m, T)]
    if mt % 2:
        spans.append((True, m - T, m - T, T))
    spans.append((False, 0, 0, mt // 2 * 3 * (T // 2)))
    return spans


def packed_rows(m, devices):
    rows = sum(span[3] for span in spans_of(m))
    unit = 8 * devices
    return -(-rows // unit) * unit


def pieces(m, total, count):
    chunk = total // count
    begin = 0
    for square, i, j, rows in spans_of(m):
        lo = begin
        while lo < begin + rows:
            hi = min(begin + rows, (lo // chunk + 1) * chunk)
            yield lo // chunk, lo % chunk, hi - lo, square, i + lo - begin, j
            lo = hi
        begin += rows
    lo = begin
    while lo < total:
        hi = (lo // chunk + 1) * chunk
        yield lo // chunk, lo % chunk, hi - lo, None, None, None
        lo = hi


def left_lanes():
    return lax.broadcasted_iota(jnp.int32, (T // 2, T), 1) < T // 2


def pack_diagonal(square, diagonal):
    h, left = T // 2, left_lanes()
    for p in range(square.shape[0] // (2 * T)):
        a, b = [square[k : k + T, k : k + T] for k in (2 * p * T, (2 * p + 1) * T)]
        at = 3 * h * p
        diagonal[at : at + h, :] = jnp.where(left, a[:h], a[h:])
        diagonal[at + h : at + 2 * h, :] = jnp.where(left, b[:h], b[h:])
        diagonal[at + 2 * h : at + 3 * h, :] = jnp.where(left, a[h:], b[:h])


def unpack_diagonal(square, diagonal):
    h, left = T // 2, left_lanes()
    for p in range(square.shape[0] // (2 * T)):
        at = 3 * h * p
        a, b, side = [diagonal[at + k * h : at + (k + 1) * h, :] for k in range(3)]
        turned = jnp.concatenate([side, side], axis=0).T
        k = 2 * p * T
        square[k : k + h, k : k + T] = jnp.where(left, a, turned[:h])
        square[k + h : k + T, k : k + T] = jnp.where(left, side, a)
        k += T
        square[k : k + h, k : k + T] = jnp.where(left, b, side)
        square[k + h : k + T, k : k + T] = jnp.where(left, turned[h:], b)


def scenario(place_fn, region, hess, flags, low_d, low_s, up_d, up_s, coup, pattern, first, rows, count):
    n, m = coup.shape
    half = jax.ShapeDtypeStruct((rows // 2, T), F32)
    return pl.pallas_call(
        functools.partial(scenario_kernel, place_fn, count),
        out_shape=(jax.ShapeDtypeStruct((n, n), F32), half, half),
        in_specs=[SMEM, HBM] + [VMEM] * 5 + [HBM, VMEM, VMEM],
        out_specs=(HBM, VMEM, VMEM),
        scratch_shapes=[
            pltpu.VMEM((n, n), F32),
            pltpu.VMEM((n, m), F32),
            pltpu.VMEM((n, n), F32),
            pltpu.VMEM((T, 2 * T), F32),
            pltpu.VMEM((T, T), BF),
            pltpu.VMEM((T, T), BF),
            pltpu.VMEM((n, n), BF),
            pltpu.VMEM((n, n), BF),
            pltpu.VMEM((n, m), BF),
            pltpu.VMEM((n, m), BF),
            pltpu.VMEM((m, m), F32),
            pltpu.VMEM((m // (2 * T) * 3 * (T // 2), T), F32),
            pltpu.SemaphoreType.DMA((2 * n // T,)),
            pltpu.SemaphoreType.DMA((n // T,)),
        ],
        compiler_params=pltpu.CompilerParams(vmem_limit_bytes=GRANT),
        name="scenario",
    )(region, *[pltpu.with_memory_space_constraint(v, pltpu.HBM) for v in (hess, flags, low_d, low_s, up_d, up_s, coup, pattern, first)])


def first_section(place_fn, parts, own, m, count):
    return pl.pallas_call(
        functools.partial(first_kernel, place_fn, count),
        out_shape=jax.ShapeDtypeStruct((own, m), F32),
        in_specs=[VMEM] * len(parts),
        out_specs=VMEM,
        scratch_shapes=[
            pltpu.VMEM((T, 2 * T), F32),
            pltpu.VMEM((m, m), BF),
            pltpu.VMEM((m, m), BF),
            pltpu.VMEM((m, m), F32),
            pltpu.VMEM((m, m), F32),
            pltpu.VMEM((m // (2 * T) * 3 * (T // 2), T), F32),
        ],
        compiler_params=pltpu.CompilerParams(vmem_limit_bytes=GRANT),
        name="first_section",
    )(*parts)


AXES = ("scen", "wide")


def swap(x, mask, count):
    return lax.ppermute(x, AXES, [(i, i ^ mask) for i in range(count)])


def rounds_of(sizes):
    (_, scen), (_, wide) = sizes
    bits = [wide << k for k in range(scen.bit_length() - 1)] + [1 << k for k in range(wide.bit_length() - 1)]
    return [bits[:1]] + [bits[k : k + 2] for k in range(1, len(bits), 2)]


def masks_of(bits):
    return [sum(b for k, b in enumerate(bits) if d >> k & 1) for d in range(1 << len(bits))]


def place_of(flat, rounds):
    bits = [bit for group in reversed(rounds) for bit in group]
    return sum(((flat // bit) % 2) << k for k, bit in enumerate(bits))


def farthest_first(n):
    return sorted(range(1, n), key=lambda k: (-k.bit_count(), k))


def sum_everywhere(x, sent, rounds, count):
    x = x + swap(sent, masks_of(rounds[0])[1], count)
    for bits in rounds[1:]:
        masks = masks_of(bits)
        part = x.shape[0] // len(masks)
        cut = [x[k * part : (k + 1) * part] for k in range(len(masks))]
        got = [swap(cut[k], masks[k], count) for k in farthest_first(len(masks))]
        x = functools.reduce(jnp.add, got, cut[0])
    parts = [x]
    for bits in reversed(rounds[1:]):
        x = parts[0] if len(parts) == 1 else jnp.concatenate(parts)
        parts = [x] + [swap(x, mask, count) for mask in masks_of(bits)[1:]]
    return parts + [swap(part, masks_of(rounds[0])[1], count) for part in parts]


def solution(mesh):
    sizes = [(axis, mesh.shape[axis]) for axis in AXES]
    count = sizes[0][1] * sizes[1][1]
    rounds = rounds_of(sizes)

    def where(first_scenario):
        scen, wide = [lax.axis_index(axis).astype(jnp.int32) for axis in AXES]
        lead = scen if first_scenario else jnp.int32(1)
        return lead, wide, place_of(scen * sizes[1][1] + wide, rounds)

    def per_device(hess_scen, flags, low_d, low_s, up_d, up_s, coupling, pattern, region, hess_first):
        own, m = hess_first.shape
        rows = packed_rows(m, count)
        factors, keep, send = [], None, None
        for i in range(hess_scen.shape[0]):
            factor, low, high = scenario(
                functools.partial(where, i == 0), region[i : i + 1], hess_scen[i],
                flags[i : i + 1], low_d[i : i + 1], low_s[i : i + 1], up_d[i : i + 1], up_s[i : i + 1],
                coupling[i], pattern[i : i + 1], hess_first, rows, count,
            )
            factors.append(factor)
            keep, send = (low, high) if keep is None else (keep + low, send + high)
        parts = sum_everywhere(keep, send, rounds, count)
        mine = first_section(functools.partial(where, True), parts, own, m, count)
        return (jnp.stack(factors), mine)

    each = P(AXES)
    return jax.shard_map(
        per_device,
        mesh=mesh,
        in_specs=(each,) * 9 + (P("wide", None),),
        out_specs=(each, P("wide", None)),
        check_vma=False,
    )
```

```python
import functools
import jax
import jax.numpy as jnp
from jax import lax
from jax.experimental import pallas as pl
from jax.experimental.pallas import tpu as pltpu
from jax.sharding import PartitionSpec as P

T = 128
Q = 32
F32 = jnp.float32
BF = jnp.bfloat16


def split(x):
    hi = x.astype(BF)
    return hi, (x - hi.astype(F32)).astype(BF)


def dot3(a, b, dims):
    ah, al = a
    bh, bl = b
    d = functools.partial(lax.dot_general, dimension_numbers=(dims, ((), ())), preferred_element_type=F32)
    return d(ah, bh) + (d(ah, bl) + d(al, bh))


NN = ((1,), (0,))
NT = ((1,), (1,))
TN = ((0,), (0,))


def row_splat(v, j):
    return jnp.broadcast_to(v[j : j + 1, :], v.shape)


def lane_splat(v, c):
    return jnp.take_along_axis(v, jnp.full((8, T), c, jnp.int32), axis=1, mode="promise_in_bounds")


def eliminate(rows, lane0):
    sub = lax.broadcasted_iota(jnp.int32, (8, T), 0)
    n = len(rows)
    v = [[r[:, i : i + T] for i in range(0, r.shape[1], T)] for r in rows]
    block = {}

    def fetch(h, k):
        block[h, k] = [lane_splat(v[h][0], lane0 + 8 * k + c) for c in range(8)]

    for h in range(n):
        fetch(h, 0)
    fetch(1, 1)
    out = []
    for g in range(n):
        for h in range(g + 1, n):
            if (h, g) not in block:
                fetch(h, g)
        later = [key for key in block if key[1] > g]
        own = block[g, g]
        pivots = jnp.zeros((8, T), F32)
        pivot = row_splat(own[0], 0)
        for j in range(8):
            pivots = jnp.where(sub == j, pivot, pivots)
            inv = 1.0 / pivot
            if j < 7:
                side = row_splat(own[j], j + 1)
                pivot = row_splat(own[j + 1], j + 1) - (side * side) * inv
            top = [row_splat(w, j) for w in v[g]]
            across = {c: row_splat(own[j], c) for c in range(j + 1, 8)}
            far = {k: [row_splat(block[k, g][j], c) for c in range(8)] for k in sorted({key[1] for key in later})}
            m = {}
            for h in range(g, n):
                here = block[h, g]
                m[h] = here[j] * inv
                for c in range(j + 1, 8):
                    here[c] = here[c] - m[h] * across[c]
            for h, k in later:
                there = block[h, k]
                for c in range(8):
                    there[c] = there[c] - m[h] * far[k][c]
            for h in range(g, n):
                part = jnp.where(sub > j, m[h], 0.0) if h == g else m[h]
                v[h] = [w - part * t for w, t in zip(v[h], top)]
        scale = lax.rsqrt(pivots)
        out.append(jnp.concatenate([w * scale for w in v[g]], axis=1))
        for h in range(g + 2, n):
            for k in (g + 1, g + 2):
                if k <= h and (h, k) not in block and (k == g + 1 or h == k):
                    fetch(h, k)
    return out


def factor_block(d_ref):
    for s in range(T // Q):
        rows = [d_ref[pl.ds(Q * s + 8 * h, 8), :] for h in range(Q // 8)]
        done = jnp.concatenate(eliminate(rows, Q * s), axis=0)
        d_ref[pl.ds(Q * s, Q), :] = done
        if s + 1 < T // Q:
            hi, lo = split(done)
            left = jnp.concatenate([hi[:, :T], hi[:, :T], lo[:, :T]], axis=0)
            right = jnp.concatenate([hi, lo, hi], axis=0)
            change = lax.dot_general(left, right, (TN, ((), ())), preferred_element_type=F32)
            below = pl.ds(Q * (s + 1), T - Q * (s + 1))
            d_ref[below, :] = d_ref[below, :] - change[Q * (s + 1) :, :]


def unit_block():
    r = lax.broadcasted_iota(jnp.int32, (T, T), 0)
    c = lax.broadcasted_iota(jnp.int32, (T, T), 1)
    return r, c


def lower_of(d_ref):
    r, c = unit_block()
    return jnp.where(c >= r, d_ref[:, :T], 0.0).T


def scenario_kernel(
    place_fn, count, outs, region, hess_hbm, flags, low_d, low_s, up_d, up_s, coup_hbm, pattern, first, factor_hbm, *refs
):
    parts = refs[:outs]
    hess, coup, factor, d_ref, ih, il, lh, ll, xh, xl, whole, diagonal, in_sem, out_sem = refs[outs:]
    n, m = coup.shape
    nt, mt = n // T, m // T
    loads = []
    for k in range(nt):
        cut = (pl.ds(k * T, n - k * T), pl.ds(k * T, T))
        loads.append(pltpu.make_async_copy(hess_hbm.at[cut], hess.at[cut], in_sem.at[k]))
        cut = pl.ds(k * T, T)
        loads.append(pltpu.make_async_copy(coup_hbm.at[cut], coup.at[cut], in_sem.at[nt + k]))
    for load in loads:
        load.start()
    stores = []
    for k in range(nt):
        cut = (slice(None), pl.ds(k * T, T))
        stores.append(pltpu.make_async_copy(factor.at[cut], factor_hbm.at[cut], out_sem.at[k]))
    lead, wide, place = place_fn()
    r, c = unit_block()
    eye = r == c
    barrier = low_d[...] / low_s[...] + flags[...].astype(F32) * up_d[...] / up_s[...]
    nb = pattern.shape[1]
    width = m // nb
    home = (lax.broadcasted_iota(jnp.int32, (1, nb), 1) == region[0]).astype(jnp.int32)
    coupled = jnp.maximum(pattern[...], home).astype(F32)
    block_row = lax.broadcasted_iota(jnp.int32, (nb, m), 0)
    column = lax.broadcasted_iota(jnp.int32, (nb, m), 1)
    spread = jnp.where((column >= block_row * width) & (column < (block_row + 1) * width), 1.0, 0.0)
    mask = jnp.dot(jnp.broadcast_to(coupled, (8, nb)), spread, preferred_element_type=F32)[0:1, :]
    for ref in (lh, ll, xh, xl, ih, il):
        ref[...] = jnp.zeros(ref.shape, BF)

    def solve(t):
        rows = pl.ds(pl.multiple_of(t * T, T), T)
        rhs = coup[rows, :] * mask - dot3((lh[rows, :], ll[rows, :]), (xh[...], xl[...]), NN)
        return rows, dot3((ih[...], il[...]), split(rhs), NN)

    def step(t, _):
        for k in range(nt):

            @pl.when(t == k)
            def _():
                lo, hi = k * T, (k + 1) * T
                loads[2 * k].wait()
                loads[2 * k + 1].wait()
                panel = hess[lo:, lo:hi]
                if k:
                    panel = panel - dot3((lh[lo:, :lo], ll[lo:, :lo]), (lh[lo:hi, :lo], ll[lo:hi, :lo]), NT)
                    factor[:lo, lo:hi] = jnp.zeros((lo, T), F32)
                d_ref[:, :T] = panel[:T] + jnp.where(eye, barrier[:, lo:hi], 0.0)
                d_ref[:, T:] = jnp.where(eye, 1.0, 0.0)
                if k + 1 < nt:
                    factor[hi:, lo:hi] = panel[T:]

        rows, solved = solve(jnp.maximum(t - 1, 0))
        xh[rows, :], xl[rows, :] = split(jnp.where(t > 0, solved, 0.0))
        factor_block(d_ref)
        ih[...], il[...] = split(d_ref[:, T:])
        for k in range(nt):

            @pl.when(t == k)
            def _():
                lo, hi = k * T, (k + 1) * T
                factor[lo:hi, lo:hi] = lower_of(d_ref)
                if k + 1 < nt:
                    below = dot3(split(factor[hi:, lo:hi]), (ih[...], il[...]), NT)
                    factor[hi:, lo:hi] = below
                    lh[hi:, lo:hi], ll[hi:, lo:hi] = split(below)
                stores[k].start()

        return 0

    lax.fori_loop(0, nt, step, 0)
    rows, solved = solve(nt - 1)
    xh[rows, :], xl[rows, :] = split(solved)
    for j in range(0, m, 2 * T):
        a = (xh[:, j:], xl[:, j:])
        b = (xh[:, j : j + 2 * T], xl[:, j : j + 2 * T])
        whole[j:, j : j + 2 * T] = dot3(a, b, TN)

    @pl.when(lead == 0)
    def _():
        own = first.shape[0]
        at = pl.ds(pl.multiple_of(wide * own, 8), own)
        whole[at, :] = whole[at, :] + first[...]

    pack_diagonal(whole, diagonal)
    each = count // outs
    chunk = parts[0].shape[0] // each
    for top in range(outs):

        @pl.when(place // each == top)
        def _():
            for l, at, rows, square, i, j in pieces(m, count * chunk, count):
                to = pl.multiple_of(((l ^ place) % each) * chunk, 8) + at
                source = whole if square else diagonal
                value = jnp.zeros((rows, T), F32) if square is None else source[i : i + rows, j : j + T]
                parts[(l // each) ^ top][pl.ds(to, rows), :] = value

    for store in stores:
        store.wait()


def first_kernel(place_fn, count, *refs):
    _, wide, place = place_fn()
    parts, (out, d_ref, lh, ll, full, work, diagonal) = refs[:-7], refs[-7:]
    m = full.shape[0]
    mt = m // T
    r, c = unit_block()
    eye = r == c
    each = count // len(parts)
    chunk = parts[0].shape[0] // each
    for top in range(len(parts)):

        @pl.when(place // each == top)
        def _():
            for l, at, rows, square, i, j in pieces(m, count * chunk, count):
                if square is not None:
                    begin = pl.multiple_of(((l ^ place) % each) * chunk, 8) + at
                    target = work if square else diagonal
                    target[i : i + rows, j : j + T] = parts[(l // each) ^ top][pl.ds(begin, rows), :]

    unpack_diagonal(work, diagonal)

    def step(t, _):
        for k in range(mt):

            @pl.when(t == k)
            def _():
                lo, hi = k * T, (k + 1) * T
                panel = work[lo:, lo:hi]
                if k:
                    panel = panel - dot3((lh[lo:, :lo], ll[lo:, :lo]), (lh[lo:hi, :lo], ll[lo:hi, :lo]), NT)
                d_ref[:, :T] = panel[:T]
                d_ref[:, T:] = jnp.where(eye, 1.0, 0.0)
                if k + 1 < mt:
                    full[hi:, lo:hi] = panel[T:]
                    full[lo:hi, hi:] = jnp.zeros((T, m - hi), F32)

        factor_block(d_ref)
        for k in range(mt):

            @pl.when(t == k)
            def _():
                lo, hi = k * T, (k + 1) * T
                full[lo:hi, lo:hi] = lower_of(d_ref)
                if k + 1 < mt:
                    below = dot3(split(full[hi:, lo:hi]), split(d_ref[:, T:]), NT)
                    full[hi:, lo:hi] = below
                    lh[hi:, lo:hi], ll[hi:, lo:hi] = split(below)

        return 0

    lax.fori_loop(0, mt, step, 0)
    own = out.shape[0]
    out[...] = full[pl.ds(pl.multiple_of(wide * own, 8), own), :]


VMEM = pl.BlockSpec(memory_space=pltpu.VMEM)
SMEM = pl.BlockSpec(memory_space=pltpu.SMEM)
HBM = pl.BlockSpec(memory_space=pltpu.HBM)
GRANT = 24 << 20


def spans_of(m):
    mt = m // T
    spans = [(True, i, j, T) for j in range(0, m, T) for i in range(j + T, m, T)]
    if mt % 2:
        spans.append((True, m - T, m - T, T))
    spans.append((False, 0, 0, mt // 2 * 3 * (T // 2)))
    return spans


def packed_rows(m, devices):
    rows = sum(span[3] for span in spans_of(m))
    unit = 8 * devices
    return -(-rows // unit) * unit


def pieces(m, total, count):
    chunk = total // count
    begin = 0
    for square, i, j, rows in spans_of(m):
        lo = begin
        while lo < begin + rows:
            hi = min(begin + rows, (lo // chunk + 1) * chunk)
            yield lo // chunk, lo % chunk, hi - lo, square, i + lo - begin, j
            lo = hi
        begin += rows
    lo = begin
    while lo < total:
        hi = (lo // chunk + 1) * chunk
        yield lo // chunk, lo % chunk, hi - lo, None, None, None
        lo = hi


def left_lanes():
    return lax.broadcasted_iota(jnp.int32, (T // 2, T), 1) < T // 2


def pack_diagonal(square, diagonal):
    h, left = T // 2, left_lanes()
    for p in range(square.shape[0] // (2 * T)):
        a, b = [square[k : k + T, k : k + T] for k in (2 * p * T, (2 * p + 1) * T)]
        at = 3 * h * p
        diagonal[at : at + h, :] = jnp.where(left, a[:h], a[h:])
        diagonal[at + h : at + 2 * h, :] = jnp.where(left, b[:h], b[h:])
        diagonal[at + 2 * h : at + 3 * h, :] = jnp.where(left, a[h:], b[:h])


def unpack_diagonal(square, diagonal):
    h, left = T // 2, left_lanes()
    for p in range(square.shape[0] // (2 * T)):
        at = 3 * h * p
        a, b, side = [diagonal[at + k * h : at + (k + 1) * h, :] for k in range(3)]
        turned = jnp.concatenate([side, side], axis=0).T
        k = 2 * p * T
        square[k : k + h, k : k + T] = jnp.where(left, a, turned[:h])
        square[k + h : k + T, k : k + T] = jnp.where(left, side, a)
        k += T
        square[k : k + h, k : k + T] = jnp.where(left, b, side)
        square[k + h : k + T, k : k + T] = jnp.where(left, turned[h:], b)


def scenario(place_fn, region, hess, flags, low_d, low_s, up_d, up_s, coup, pattern, first, rows, count, outs):
    n, m = coup.shape
    part = jax.ShapeDtypeStruct((rows // outs, T), F32)
    return pl.pallas_call(
        functools.partial(scenario_kernel, place_fn, count, outs),
        out_shape=(jax.ShapeDtypeStruct((n, n), F32),) + (part,) * outs,
        in_specs=[SMEM, HBM] + [VMEM] * 5 + [HBM, VMEM, VMEM],
        out_specs=(HBM,) + (VMEM,) * outs,
        scratch_shapes=[
            pltpu.VMEM((n, n), F32),
            pltpu.VMEM((n, m), F32),
            pltpu.VMEM((n, n), F32),
            pltpu.VMEM((T, 2 * T), F32),
            pltpu.VMEM((T, T), BF),
            pltpu.VMEM((T, T), BF),
            pltpu.VMEM((n, n), BF),
            pltpu.VMEM((n, n), BF),
            pltpu.VMEM((n, m), BF),
            pltpu.VMEM((n, m), BF),
            pltpu.VMEM((m, m), F32),
            pltpu.VMEM((m // (2 * T) * 3 * (T // 2), T), F32),
            pltpu.SemaphoreType.DMA((2 * n // T,)),
            pltpu.SemaphoreType.DMA((n // T,)),
        ],
        compiler_params=pltpu.CompilerParams(vmem_limit_bytes=GRANT),
        name="scenario",
    )(region, *[pltpu.with_memory_space_constraint(v, pltpu.HBM) for v in (hess, flags, low_d, low_s, up_d, up_s, coup, pattern, first)])


def first_section(place_fn, parts, own, m, count):
    return pl.pallas_call(
        functools.partial(first_kernel, place_fn, count),
        out_shape=jax.ShapeDtypeStruct((own, m), F32),
        in_specs=[VMEM] * len(parts),
        out_specs=VMEM,
        scratch_shapes=[
            pltpu.VMEM((T, 2 * T), F32),
            pltpu.VMEM((m, m), BF),
            pltpu.VMEM((m, m), BF),
            pltpu.VMEM((m, m), F32),
            pltpu.VMEM((m, m), F32),
            pltpu.VMEM((m // (2 * T) * 3 * (T // 2), T), F32),
        ],
        compiler_params=pltpu.CompilerParams(vmem_limit_bytes=GRANT),
        name="first_section",
    )(*parts)


AXES = ("scen", "wide")


def swap(x, mask, count):
    return lax.ppermute(x, AXES, [(i, i ^ mask) for i in range(count)])


def rounds_of(sizes):
    (_, scen), (_, wide) = sizes
    bits = [wide << k for k in range(scen.bit_length() - 1)] + [1 << k for k in range(wide.bit_length() - 1)]
    return [bits[:1]] + [bits[k : k + 2] for k in range(1, len(bits), 2)]


def masks_of(bits):
    return [sum(b for k, b in enumerate(bits) if d >> k & 1) for d in range(1 << len(bits))]


def place_of(flat, rounds):
    bits = [bit for group in reversed(rounds) for bit in group]
    return sum(((flat // bit) % 2) << k for k, bit in enumerate(bits))


def farthest_first(n):
    return sorted(range(1, n), key=lambda k: (-k.bit_count(), k))


def sum_everywhere(kept, sent, rounds, count):
    order = farthest_first(len(kept)) + [0]
    cut = {k: kept[k] + swap(sent[k], masks_of(rounds[0])[1], count) for k in order}
    for step, bits in enumerate(rounds[1:]):
        masks = masks_of(bits)
        if step:
            part = x.shape[0] // len(masks)
            cut = [x[k * part : (k + 1) * part] for k in range(len(masks))]
        got = [swap(cut[k], masks[k], count) for k in farthest_first(len(masks))]
        x = functools.reduce(jnp.add, got, cut[0])
    parts = [x]
    for bits in reversed(rounds[1:]):
        x = parts[0] if len(parts) == 1 else jnp.concatenate(parts)
        parts = [x] + [swap(x, mask, count) for mask in masks_of(bits)[1:]]
    return parts + [swap(part, masks_of(rounds[0])[1], count) for part in parts]


def solution(mesh):
    sizes = [(axis, mesh.shape[axis]) for axis in AXES]
    count = sizes[0][1] * sizes[1][1]
    rounds = rounds_of(sizes)

    def where(first_scenario):
        scen, wide = [lax.axis_index(axis).astype(jnp.int32) for axis in AXES]
        lead = scen if first_scenario else jnp.int32(1)
        return lead, wide, place_of(scen * sizes[1][1] + wide, rounds)

    def per_device(hess_scen, flags, low_d, low_s, up_d, up_s, coupling, pattern, region, hess_first):
        own, m = hess_first.shape
        rows = packed_rows(m, count)
        outs = 2 * len(masks_of(rounds[1]))
        factors, parts = [], None
        for i in range(hess_scen.shape[0]):
            factor, *new = scenario(
                functools.partial(where, i == 0), region[i : i + 1], hess_scen[i],
                flags[i : i + 1], low_d[i : i + 1], low_s[i : i + 1], up_d[i : i + 1], up_s[i : i + 1],
                coupling[i], pattern[i : i + 1], hess_first, rows, count, outs,
            )
            factors.append(factor)
            parts = new if parts is None else [a + b for a, b in zip(parts, new)]
        parts = sum_everywhere(parts[: outs // 2], parts[outs // 2 :], rounds, count)
        mine = first_section(functools.partial(where, True), parts, own, m, count)
        return (jnp.stack(factors), mine)

    each = P(AXES)
    return jax.shard_map(
        per_device,
        mesh=mesh,
        in_specs=(each,) * 9 + (P("wide", None),),
        out_specs=(each, P("wide", None)),
        check_vma=False,
    )
```

```python
import functools
import jax
import jax.numpy as jnp
from jax import lax
from jax.experimental import pallas as pl
from jax.experimental.pallas import tpu as pltpu
from jax.sharding import PartitionSpec as P

T = 128
Q = 32
F32 = jnp.float32
BF = jnp.bfloat16


def split(x):
    hi = x.astype(BF)
    return hi, (x - hi.astype(F32)).astype(BF)


def dot3(a, b, dims):
    ah, al = a
    bh, bl = b
    d = functools.partial(lax.dot_general, dimension_numbers=(dims, ((), ())), preferred_element_type=F32)
    return d(ah, bh) + (d(ah, bl) + d(al, bh))


def dot3_stacked(a, b, dims):
    (ah, al), (bh, bl), ((ka,), (kb,)) = a, b, dims
    left = jnp.concatenate([ah, ah, al], axis=ka)
    right = jnp.concatenate([bh, bl, bh], axis=kb)
    return lax.dot_general(left, right, (dims, ((), ())), preferred_element_type=F32)


NN = ((1,), (0,))
NT = ((1,), (1,))
TN = ((0,), (0,))


def row_splat(v, j):
    return jnp.broadcast_to(v[j : j + 1, :], v.shape)


def lane_splat(v, c):
    return jnp.take_along_axis(v, jnp.full((8, T), c, jnp.int32), axis=1, mode="promise_in_bounds")


def eliminate(rows, lane0):
    sub = lax.broadcasted_iota(jnp.int32, (8, T), 0)
    n = len(rows)
    v = [[r[:, i : i + T] for i in range(0, r.shape[1], T)] for r in rows]
    block = {}

    def fetch(h, k):
        block[h, k] = [lane_splat(v[h][0], lane0 + 8 * k + c) for c in range(8)]

    for h in range(n):
        fetch(h, 0)
    fetch(1, 1)
    out = []
    for g in range(n):
        for h in range(g + 1, n):
            if (h, g) not in block:
                fetch(h, g)
        later = [key for key in block if key[1] > g]
        own = block[g, g]
        pivots = jnp.zeros((8, T), F32)
        pivot = row_splat(own[0], 0)
        for j in range(8):
            pivots = jnp.where(sub == j, pivot, pivots)
            inv = 1.0 / pivot
            if j < 7:
                side = row_splat(own[j], j + 1)
                pivot = row_splat(own[j + 1], j + 1) - (side * side) * inv
            top = [row_splat(w, j) for w in v[g]]
            across = {c: row_splat(own[j], c) for c in range(j + 1, 8)}
            far = {k: [row_splat(block[k, g][j], c) for c in range(8)] for k in sorted({key[1] for key in later})}
            m = {}
            for h in range(g, n):
                here = block[h, g]
                m[h] = here[j] * inv
                for c in range(j + 1, 8):
                    here[c] = here[c] - m[h] * across[c]
            for h, k in later:
                there = block[h, k]
                for c in range(8):
                    there[c] = there[c] - m[h] * far[k][c]
            for h in range(g, n):
                part = jnp.where(sub > j, m[h], 0.0) if h == g else m[h]
                v[h] = [w - part * t for w, t in zip(v[h], top)]
        scale = lax.rsqrt(pivots)
        out.append(jnp.concatenate([w * scale for w in v[g]], axis=1))
        for h in range(g + 2, n):
            for k in (g + 1, g + 2):
                if k <= h and (h, k) not in block and (k == g + 1 or h == k):
                    fetch(h, k)
    return out


def factor_block(d_ref):
    for s in range(T // Q):
        rows = [d_ref[pl.ds(Q * s + 8 * h, 8), :] for h in range(Q // 8)]
        done = jnp.concatenate(eliminate(rows, Q * s), axis=0)
        d_ref[pl.ds(Q * s, Q), :] = done
        if s + 1 < T // Q:
            hi, lo = split(done)
            left = jnp.concatenate([hi[:, :T], hi[:, :T], lo[:, :T]], axis=0)
            right = jnp.concatenate([hi, lo, hi], axis=0)
            change = lax.dot_general(left, right, (TN, ((), ())), preferred_element_type=F32)
            below = pl.ds(Q * (s + 1), T - Q * (s + 1))
            d_ref[below, :] = d_ref[below, :] - change[Q * (s + 1) :, :]


def unit_block():
    r = lax.broadcasted_iota(jnp.int32, (T, T), 0)
    c = lax.broadcasted_iota(jnp.int32, (T, T), 1)
    return r, c


def lower_of(d_ref):
    r, c = unit_block()
    return jnp.where(c >= r, d_ref[:, :T], 0.0).T


def scenario_kernel(
    place_fn, count, outs, region, hess_hbm, flags, low_d, low_s, up_d, up_s, coup_hbm, pattern, first, factor_hbm, *refs
):
    parts = refs[:outs]
    hess, coup, factor, d_ref, ih, il, lh, ll, xh, xl, whole, diagonal, in_sem, out_sem = refs[outs:]
    n, m = coup.shape
    nt, mt = n // T, m // T
    loads = []
    for k in range(nt):
        cut = (pl.ds(k * T, n - k * T), pl.ds(k * T, T))
        loads.append(pltpu.make_async_copy(hess_hbm.at[cut], hess.at[cut], in_sem.at[k]))
        cut = pl.ds(k * T, T)
        loads.append(pltpu.make_async_copy(coup_hbm.at[cut], coup.at[cut], in_sem.at[nt + k]))
    for load in loads:
        load.start()
    stores = []
    for k in range(nt):
        cut = (slice(None), pl.ds(k * T, T))
        stores.append(pltpu.make_async_copy(factor.at[cut], factor_hbm.at[cut], out_sem.at[k]))
    lead, wide, place = place_fn()
    r, c = unit_block()
    eye = r == c
    barrier = low_d[...] / low_s[...] + flags[...].astype(F32) * up_d[...] / up_s[...]
    nb = pattern.shape[1]
    width = m // nb
    home = (lax.broadcasted_iota(jnp.int32, (1, nb), 1) == region[0]).astype(jnp.int32)
    coupled = jnp.maximum(pattern[...], home).astype(F32)
    block_row = lax.broadcasted_iota(jnp.int32, (nb, m), 0)
    column = lax.broadcasted_iota(jnp.int32, (nb, m), 1)
    spread = jnp.where((column >= block_row * width) & (column < (block_row + 1) * width), 1.0, 0.0)
    mask = jnp.dot(jnp.broadcast_to(coupled, (8, nb)), spread, preferred_element_type=F32)[0:1, :]
    for ref in (lh, ll, xh, xl, ih, il):
        ref[...] = jnp.zeros(ref.shape, BF)

    def solve(t):
        rows = pl.ds(pl.multiple_of(t * T, T), T)
        rhs = coup[rows, :] * mask - dot3((lh[rows, :], ll[rows, :]), (xh[...], xl[...]), NN)
        return rows, dot3((ih[...], il[...]), split(rhs), NN)

    def step(t, _):
        for k in range(nt):

            @pl.when(t == k)
            def _():
                lo, hi = k * T, (k + 1) * T
                loads[2 * k].wait()
                loads[2 * k + 1].wait()
                panel = hess[lo:, lo:hi]
                if k:
                    panel = panel - dot3((lh[lo:, :lo], ll[lo:, :lo]), (lh[lo:hi, :lo], ll[lo:hi, :lo]), NT)
                    factor[:lo, lo:hi] = jnp.zeros((lo, T), F32)
                d_ref[:, :T] = panel[:T] + jnp.where(eye, barrier[:, lo:hi], 0.0)
                d_ref[:, T:] = jnp.where(eye, 1.0, 0.0)
                if k + 1 < nt:
                    factor[hi:, lo:hi] = panel[T:]

        rows, solved = solve(jnp.maximum(t - 1, 0))
        xh[rows, :], xl[rows, :] = split(jnp.where(t > 0, solved, 0.0))
        factor_block(d_ref)
        ih[...], il[...] = split(d_ref[:, T:])
        for k in range(nt):

            @pl.when(t == k)
            def _():
                lo, hi = k * T, (k + 1) * T
                factor[lo:hi, lo:hi] = lower_of(d_ref)
                if k + 1 < nt:
                    below = dot3(split(factor[hi:, lo:hi]), (ih[...], il[...]), NT)
                    factor[hi:, lo:hi] = below
                    lh[hi:, lo:hi], ll[hi:, lo:hi] = split(below)
                stores[k].start()

        return 0

    lax.fori_loop(0, nt, step, 0)
    rows, solved = solve(nt - 1)
    xh[rows, :], xl[rows, :] = split(solved)
    for j in range(0, m, 2 * T):
        a = (xh[:, j:], xl[:, j:])
        b = (xh[:, j : j + 2 * T], xl[:, j : j + 2 * T])
        whole[j:, j : j + 2 * T] = dot3(a, b, TN)

    @pl.when(lead == 0)
    def _():
        own = first.shape[0]
        at = pl.ds(pl.multiple_of(wide * own, 8), own)
        whole[at, :] = whole[at, :] + first[...]

    pack_diagonal(whole, diagonal)
    each = count // outs
    chunk = parts[0].shape[0] // each
    for top in range(outs):

        @pl.when(place // each == top)
        def _():
            for l, at, rows, square, i, j in pieces(m, count * chunk, count):
                to = pl.multiple_of(((l ^ place) % each) * chunk, 8) + at
                source = whole if square else diagonal
                value = jnp.zeros((rows, T), F32) if square is None else source[i : i + rows, j : j + T]
                parts[(l // each) ^ top][pl.ds(to, rows), :] = value

    for store in stores:
        store.wait()


def first_kernel(place_fn, count, *refs):
    _, wide, place = place_fn()
    parts, (out, d_ref, lh, ll, full, work, diagonal) = refs[:-7], refs[-7:]
    m = full.shape[0]
    mt = m // T
    r, c = unit_block()
    eye = r == c
    each = count // len(parts)
    chunk = parts[0].shape[0] // each
    for top in range(len(parts)):

        @pl.when(place // each == top)
        def _():
            for l, at, rows, square, i, j in pieces(m, count * chunk, count):
                if square is not None:
                    begin = pl.multiple_of(((l ^ place) % each) * chunk, 8) + at
                    target = work if square else diagonal
                    target[i : i + rows, j : j + T] = parts[(l // each) ^ top][pl.ds(begin, rows), :]

    unpack_diagonal(work, diagonal)

    def step(t, _):
        for k in range(mt):

            @pl.when(t == k)
            def _():
                lo, hi = k * T, (k + 1) * T
                panel = work[lo:, lo:hi]
                if k:
                    panel = panel - dot3_stacked((lh[lo:, :lo], ll[lo:, :lo]), (lh[lo:hi, :lo], ll[lo:hi, :lo]), NT)
                d_ref[:, :T] = panel[:T]
                d_ref[:, T:] = jnp.where(eye, 1.0, 0.0)
                if k + 1 < mt:
                    full[hi:, lo:hi] = panel[T:]
                    full[lo:hi, hi:] = jnp.zeros((T, m - hi), F32)

        factor_block(d_ref)
        for k in range(mt):

            @pl.when(t == k)
            def _():
                lo, hi = k * T, (k + 1) * T
                full[lo:hi, lo:hi] = lower_of(d_ref)
                if k + 1 < mt:
                    below = dot3_stacked(split(full[hi:, lo:hi]), split(d_ref[:, T:]), NT)
                    full[hi:, lo:hi] = below
                    lh[hi:, lo:hi], ll[hi:, lo:hi] = split(below)

        return 0

    lax.fori_loop(0, mt, step, 0)
    own = out.shape[0]
    out[...] = full[pl.ds(pl.multiple_of(wide * own, 8), own), :]


VMEM = pl.BlockSpec(memory_space=pltpu.VMEM)
SMEM = pl.BlockSpec(memory_space=pltpu.SMEM)
HBM = pl.BlockSpec(memory_space=pltpu.HBM)
GRANT = 24 << 20


def spans_of(m):
    mt = m // T
    spans = [(True, i, j, T) for j in range(0, m, T) for i in range(j + T, m, T)]
    if mt % 2:
        spans.append((True, m - T, m - T, T))
    spans.append((False, 0, 0, mt // 2 * 3 * (T // 2)))
    return spans


def packed_rows(m, devices):
    rows = sum(span[3] for span in spans_of(m))
    unit = 8 * devices
    return -(-rows // unit) * unit


def pieces(m, total, count):
    chunk = total // count
    begin = 0
    for square, i, j, rows in spans_of(m):
        lo = begin
        while lo < begin + rows:
            hi = min(begin + rows, (lo // chunk + 1) * chunk)
            yield lo // chunk, lo % chunk, hi - lo, square, i + lo - begin, j
            lo = hi
        begin += rows
    lo = begin
    while lo < total:
        hi = (lo // chunk + 1) * chunk
        yield lo // chunk, lo % chunk, hi - lo, None, None, None
        lo = hi


def left_lanes():
    return lax.broadcasted_iota(jnp.int32, (T // 2, T), 1) < T // 2


def pack_diagonal(square, diagonal):
    h, left = T // 2, left_lanes()
    for p in range(square.shape[0] // (2 * T)):
        a, b = [square[k : k + T, k : k + T] for k in (2 * p * T, (2 * p + 1) * T)]
        at = 3 * h * p
        diagonal[at : at + h, :] = jnp.where(left, a[:h], a[h:])
        diagonal[at + h : at + 2 * h, :] = jnp.where(left, b[:h], b[h:])
        diagonal[at + 2 * h : at + 3 * h, :] = jnp.where(left, a[h:], b[:h])


def unpack_diagonal(square, diagonal):
    h, left = T // 2, left_lanes()
    for p in range(square.shape[0] // (2 * T)):
        at = 3 * h * p
        a, b, side = [diagonal[at + k * h : at + (k + 1) * h, :] for k in range(3)]
        turned = jnp.concatenate([side, side], axis=0).T
        k = 2 * p * T
        square[k : k + h, k : k + T] = jnp.where(left, a, turned[:h])
        square[k + h : k + T, k : k + T] = jnp.where(left, side, a)
        k += T
        square[k : k + h, k : k + T] = jnp.where(left, b, side)
        square[k + h : k + T, k : k + T] = jnp.where(left, turned[h:], b)


def scenario(place_fn, region, hess, flags, low_d, low_s, up_d, up_s, coup, pattern, first, rows, count, outs):
    n, m = coup.shape
    part = jax.ShapeDtypeStruct((rows // outs, T), F32)
    return pl.pallas_call(
        functools.partial(scenario_kernel, place_fn, count, outs),
        out_shape=(jax.ShapeDtypeStruct((n, n), F32),) + (part,) * outs,
        in_specs=[SMEM, HBM] + [VMEM] * 5 + [HBM, VMEM, VMEM],
        out_specs=(HBM,) + (VMEM,) * outs,
        scratch_shapes=[
            pltpu.VMEM((n, n), F32),
            pltpu.VMEM((n, m), F32),
            pltpu.VMEM((n, n), F32),
            pltpu.VMEM((T, 2 * T), F32),
            pltpu.VMEM((T, T), BF),
            pltpu.VMEM((T, T), BF),
            pltpu.VMEM((n, n), BF),
            pltpu.VMEM((n, n), BF),
            pltpu.VMEM((n, m), BF),
            pltpu.VMEM((n, m), BF),
            pltpu.VMEM((m, m), F32),
            pltpu.VMEM((m // (2 * T) * 3 * (T // 2), T), F32),
            pltpu.SemaphoreType.DMA((2 * n // T,)),
            pltpu.SemaphoreType.DMA((n // T,)),
        ],
        compiler_params=pltpu.CompilerParams(vmem_limit_bytes=GRANT),
        name="scenario",
    )(region, *[pltpu.with_memory_space_constraint(v, pltpu.HBM) for v in (hess, flags, low_d, low_s, up_d, up_s, coup, pattern, first)])


def first_section(place_fn, parts, own, m, count):
    return pl.pallas_call(
        functools.partial(first_kernel, place_fn, count),
        out_shape=jax.ShapeDtypeStruct((own, m), F32),
        in_specs=[VMEM] * len(parts),
        out_specs=VMEM,
        scratch_shapes=[
            pltpu.VMEM((T, 2 * T), F32),
            pltpu.VMEM((m, m), BF),
            pltpu.VMEM((m, m), BF),
            pltpu.VMEM((m, m), F32),
            pltpu.VMEM((m, m), F32),
            pltpu.VMEM((m // (2 * T) * 3 * (T // 2), T), F32),
        ],
        compiler_params=pltpu.CompilerParams(vmem_limit_bytes=GRANT),
        name="first_section",
    )(*parts)


AXES = ("scen", "wide")


def swap(x, mask, count):
    return lax.ppermute(x, AXES, [(i, i ^ mask) for i in range(count)])


def rounds_of(sizes):
    (_, scen), (_, wide) = sizes
    bits = [wide << k for k in range(scen.bit_length() - 1)] + [1 << k for k in range(wide.bit_length() - 1)]
    return [bits[:1]] + [bits[k : k + 2] for k in range(1, len(bits), 2)]


def masks_of(bits):
    return [sum(b for k, b in enumerate(bits) if d >> k & 1) for d in range(1 << len(bits))]


def place_of(flat, rounds):
    bits = [bit for group in reversed(rounds) for bit in group]
    return sum(((flat // bit) % 2) << k for k, bit in enumerate(bits))


def farthest_first(n):
    return sorted(range(1, n), key=lambda k: (-k.bit_count(), k))


def sum_everywhere(kept, sent, rounds, count):
    order = list(range(len(kept)))[::-1]
    cut = {k: kept[k] + swap(sent[k], masks_of(rounds[0])[1], count) for k in order}
    for step, bits in enumerate(rounds[1:]):
        masks = masks_of(bits)
        if step:
            part = x.shape[0] // len(masks)
            cut = [x[k * part : (k + 1) * part] for k in range(len(masks))]
        got = [swap(cut[k], masks[k], count) for k in (farthest_first(len(masks)) if step else order[:-1])]
        x = functools.reduce(jnp.add, got, cut[0])
    parts = [x]
    for bits in reversed(rounds[1:]):
        x = parts[0] if len(parts) == 1 else jnp.concatenate(parts)
        parts = [x] + [swap(x, mask, count) for mask in masks_of(bits)[1:]]
    return parts + [swap(part, masks_of(rounds[0])[1], count) for part in parts]


def solution(mesh):
    sizes = [(axis, mesh.shape[axis]) for axis in AXES]
    count = sizes[0][1] * sizes[1][1]
    rounds = rounds_of(sizes)

    def where(first_scenario):
        scen, wide = [lax.axis_index(axis).astype(jnp.int32) for axis in AXES]
        lead = scen if first_scenario else jnp.int32(1)
        return lead, wide, place_of(scen * sizes[1][1] + wide, rounds)

    def per_device(hess_scen, flags, low_d, low_s, up_d, up_s, coupling, pattern, region, hess_first):
        own, m = hess_first.shape
        rows = packed_rows(m, count)
        outs = 2 * len(masks_of(rounds[1]))
        factors, parts = [], None
        for i in range(hess_scen.shape[0]):
            factor, *new = scenario(
                functools.partial(where, i == 0), region[i : i + 1], hess_scen[i],
                flags[i : i + 1], low_d[i : i + 1], low_s[i : i + 1], up_d[i : i + 1], up_s[i : i + 1],
                coupling[i], pattern[i : i + 1], hess_first, rows, count, outs,
            )
            factors.append(factor)
            parts = new if parts is None else [a + b for a, b in zip(parts, new)]
        parts = sum_everywhere(parts[: outs // 2], parts[outs // 2 :], rounds, count)
        mine = first_section(functools.partial(where, True), parts, own, m, count)
        return (jnp.stack(factors), mine)

    each = P(AXES)
    return jax.shard_map(
        per_device,
        mesh=mesh,
        in_specs=(each,) * 9 + (P("wide", None),),
        out_specs=(each, P("wide", None)),
        check_vma=False,
    )
```
